256 devices in a mesh: seq: 64 (over y, z, core), mp: 4 (over x).
Axes of the slice: x: 4, y: 4, z: 8, core: 2. Of those that a mesh axis runs over, the one named last changes fastest.
Arguments:
- tokens: bfloat16 [8192, 3584], P('seq'), may hold values from -6 to 6
- query_weight: bfloat16 [3584, 4096], P('seq', 'mp'), may hold values from -0.09375 to 0.09375
- key_weight: bfloat16 [3584, 4096], P('seq', 'mp'), may hold values from -0.09375 to 0.09375
- value_weight: bfloat16 [3584, 4096], P('seq', 'mp'), may hold values from -0.09375 to 0.09375
- adapter_down_maps: bfloat16 [3584, 128], replicated, may hold values from -0.09375 to 0.09375
- lifting_matrices: bfloat16 [2, 64, 4096], P(None, None, 'mp'), may hold values from -0.75 to 0.75
- decay_logarithms: float32 [32, 8192], P('mp', 'seq'), may hold values from -1 to 0, as said below
- output_gradient: bfloat16 [8192, 4096], P('seq', 'mp'), may hold values from -0.06591797 to 0.06591797
Outputs:
- grad_down: float32 [3584, 128], P(('seq', 'mp'))
- grad_up: float32 [2, 64, 4096], P(None, None, 'mp')
The draws below stay inside these ranges and needn't reach their ends.
Inputs may be any that keep to these rules, and one draw needn't show every extreme that they name: `decay_logarithms`: every entry is negative.
All inputs are finite; a program needn't handle non-finite values.
Results may differ from the reference program's by a relative error of at most 0.006.
Values may be sent and summed in bfloat16 or wider, within the bound.
No kernel may reach another device: no remote copies, remote signals or barrier semaphores. Data moves between devices by JAX's collectives and lax.ppermute only.
A program may use at most 192 MiB of HBM per device.

```python
import math
import jax
import jax.numpy as jnp
from jax import lax

MODEL_WIDTH = 3584
HEADS = 32
HK = 128
ADAPTER_RANK = 64
TOK_DEV = 128
STREAM_LENGTH = 8192
HEAD_FEATURES = 4096


def draw_decay_logarithms(key, part):
    keys = jax.random.split(jax.random.fold_in(key, 7103), 8)
    slow_share = 0.5
    slow = jax.random.uniform(keys[0], (HEADS,), jnp.float32) < slow_share
    slow_rate = jnp.exp(jax.random.uniform(keys[1], (HEADS,), jnp.float32, math.log(0.02), math.log(0.2))) * 2.302585 / STREAM_LENGTH
    fast_rate = jnp.exp(jax.random.uniform(keys[2], (HEADS,), jnp.float32, math.log(1.0 / 50.0), math.log(1.0 / 30.0)))
    base = jnp.where(slow, slow_rate, fast_rate)
    nblocks = STREAM_LENGTH // TOK_DEV
    block_factor = jnp.exp(jax.random.uniform(keys[3], (HEADS, nblocks, 1), jnp.float32, math.log(0.4), 0.0))
    block_factor = jnp.broadcast_to(block_factor, (HEADS, nblocks, TOK_DEV)).reshape(HEADS, STREAM_LENGTH)
    token_factor = jnp.exp(jax.random.uniform(keys[4], (HEADS, STREAM_LENGTH), jnp.float32, math.log(0.5), math.log(1.5)))
    fading_speed = base[:, None] * block_factor * token_factor
    first_offset = jax.random.randint(keys[5], (HEADS, 1), 0, STREAM_LENGTH)
    second_offset = (first_offset + jax.random.randint(keys[7], (HEADS, 1), 1, STREAM_LENGTH)) % STREAM_LENGTH
    step_offsets = jnp.concatenate([first_offset, second_offset], axis=1)
    stack_level = jax.random.uniform(keys[6], (HEADS, 2), jnp.float32, math.log(0.5), math.log(0.8))
    spike_placement = jnp.arange(STREAM_LENGTH)[None, None, :] == step_offsets[:, :, None]
    spike_clusters = jnp.sum(jnp.where(spike_placement, stack_level[:, :, None], 0.0), axis=1)
    return (spike_clusters - fading_speed).astype(jnp.float32)


def level_of(rng, dims, cuts, smallest, high):
    factor_of, own = 1.0, jax.random.fold_in(rng, 6)
    for position, shards_of in cuts:
        draws = jnp.exp(jax.random.uniform(jax.random.fold_in(own, position), (shards_of,), jnp.float32, smallest / len(cuts), high / len(cuts)))
        factor_of = factor_of * jnp.repeat(draws, dims[position] // shards_of).reshape([-1 if axis == position else 1 for axis in range(len(dims))])
    return factor_of


def normal_values(key, shape, deviation, bound, shards=(), held_as=jnp.bfloat16):
    level = level_of(key, shape, shards, -0.22, 0.18) if shards else 1.0
    drawn = jax.random.normal(key, shape, jnp.float32) * deviation * level
    return jnp.minimum(jnp.maximum(drawn, -bound), bound).astype(held_as)


def setup_inputs(seed: int = 0) -> dict:
    seeds = jax.random.split(jax.random.key(seed), 9)
    return {
        "tokens": normal_values(seeds[0], (STREAM_LENGTH, MODEL_WIDTH), 1.0, 6.0, ((0, 64),)),
        "query_weight": normal_values(seeds[1], (MODEL_WIDTH, HEAD_FEATURES), MODEL_WIDTH ** -0.5, 0.09375, ((0, 64), (1, 4))),
        "key_weight": normal_values(seeds[2], (MODEL_WIDTH, HEAD_FEATURES), MODEL_WIDTH ** -0.5, 0.09375, ((0, 64), (1, 4))),
        "value_weight": normal_values(seeds[3], (MODEL_WIDTH, HEAD_FEATURES), MODEL_WIDTH ** -0.5, 0.09375, ((0, 64), (1, 4))),
        "adapter_down_maps": normal_values(seeds[4], (MODEL_WIDTH, 2 * ADAPTER_RANK), MODEL_WIDTH ** -0.5, 0.09375),
        "lifting_matrices": normal_values(seeds[5], (2, ADAPTER_RANK, HEAD_FEATURES), ADAPTER_RANK ** -0.5, 0.75, ((2, 4),)),
        "decay_logarithms": draw_decay_logarithms(jax.random.fold_in(seeds[8], 71), 0),
        "output_gradient": normal_values(seeds[7], (STREAM_LENGTH, HEAD_FEATURES), (STREAM_LENGTH ** -0.5), 0.06591797, ((0, 64), (1, 4))),
    }


adapter_scale = 2.0
eps_norm = 1e-06
exact_arithmetic = lax.Precision.HIGHEST

def split_heads(flat):
    return flat.reshape(flat.shape[0], HEADS, HK).transpose(1, 0, 2)

def join_heads(arr):
    return arr.transpose(1, 0, 2).reshape(arr.shape[1], HEADS * HK)

def round_half(arr):
    return lax.optimization_barrier(arr.astype(jnp.bfloat16)).astype(jnp.float32)

def decay_terms(decay_block):
    cumulative = jnp.cumsum(decay_block, axis=1)
    total = cumulative[:, -1]
    gain = jnp.exp(total)
    tail = jnp.exp(total[:, None] - cumulative)
    lead = jnp.exp(cumulative)
    length = decay_block.shape[1]
    causal = jnp.arange(length)[:, None] >= jnp.arange(length)[None, :]
    spread = cumulative[:, :, None] - cumulative[:, None, :]
    decay_mat = jnp.where(causal[None], jnp.exp(jnp.where(causal[None], spread, 0.0)), 0.0)
    return (gain, tail, lead, decay_mat)

def reference(tokens, query_weight, key_weight, value_weight, adapter_down_maps, lifting_matrices, decay_logarithms, output_gradient):
    blocks = jnp.arange(STREAM_LENGTH // TOK_DEV, dtype=jnp.int32)

    def inputs_of(index):
        start = (index * TOK_DEV).astype(jnp.int32)
        input_rows = lax.dynamic_slice_in_dim(tokens, start, TOK_DEV, 0)
        decay_block = lax.dynamic_slice_in_dim(decay_logarithms, start, TOK_DEV, 1)
        low_product = jnp.dot(input_rows, adapter_down_maps, preferred_element_type=jnp.float32).astype(jnp.bfloat16)
        return (start, input_rows, decay_block, low_product)

    def keys_values(input_rows, low_product):
        key_pre = jnp.dot(input_rows, key_weight, preferred_element_type=jnp.float32)
        value_before_norm = jnp.dot(input_rows, value_weight, preferred_element_type=jnp.float32) + adapter_scale * jnp.dot(low_product[:, ADAPTER_RANK:], lifting_matrices[1], preferred_element_type=jnp.float32)
        key_f = split_heads(jax.nn.silu(key_pre).astype(jnp.bfloat16)).astype(jnp.float32)
        value_f = split_heads(value_before_norm.astype(jnp.bfloat16)).astype(jnp.float32)
        return (key_f, value_f)

    def forward_step(state, index):
        start, input_rows, decay_block, low_product = inputs_of(index)
        key_f, value_f = keys_values(input_rows, low_product)
        gain, tail, lead, decay_mat = decay_terms(decay_block)
        local = jnp.einsum('hsi,hsj->hij', key_f * tail[:, :, None], value_f, precision=exact_arithmetic)
        return (gain[:, None, None] * state + local, state)
    zero_state = jnp.zeros((HEADS, HK, HK), jnp.float32)
    _, states = lax.scan(forward_step, zero_state, blocks)

    def backward_step(carry, inputs):
        later, grad_down, grad_up = carry
        index, state_in = inputs
        start, input_rows, decay_block, low_product = inputs_of(index)
        key_f, value_f = keys_values(input_rows, low_product)
        gain, tail, lead, decay_mat = decay_terms(decay_block)
        query_before_norm = jnp.dot(input_rows, query_weight, preferred_element_type=jnp.float32) + adapter_scale * jnp.dot(low_product[:, :ADAPTER_RANK], lifting_matrices[0], preferred_element_type=jnp.float32)
        query_f = split_heads(jax.nn.silu(query_before_norm).astype(jnp.bfloat16)).astype(jnp.float32)
        scores = jnp.einsum('htd,hsd->hts', query_f, key_f, precision=exact_arithmetic)
        mixed = round_half(scores * decay_mat)
        attn = jnp.einsum('hts,hsj->htj', mixed, value_f, precision=exact_arithmetic) + lead[:, :, None] * jnp.einsum('hti,hij->htj', query_f, state_in, precision=exact_arithmetic)
        rms = jnp.sqrt(lax.optimization_barrier(jnp.mean(attn * attn, axis=-1, keepdims=True)) + eps_norm)
        normed = attn / rms
        upstream = split_heads(lax.dynamic_slice_in_dim(output_gradient, start, TOK_DEV, 0).astype(jnp.float32))
        d_attn = (upstream - normed * lax.optimization_barrier(jnp.mean(upstream * normed, axis=-1, keepdims=True))) / rms
        d_attn_b = round_half(d_attn)
        carried = jnp.einsum('hti,htj->hij', query_f * lead[:, :, None], d_attn, precision=exact_arithmetic)
        d_mixed = round_half(jnp.einsum('htj,hsj->hts', d_attn_b, value_f, precision=exact_arithmetic) * decay_mat)
        d_query = jnp.einsum('hts,hsi->hti', d_mixed, key_f, precision=exact_arithmetic) + lead[:, :, None] * jnp.einsum('htj,hij->hti', d_attn, state_in, precision=exact_arithmetic)
        d_value = jnp.einsum('hts,htj->hsj', mixed, d_attn_b, precision=exact_arithmetic) + tail[:, :, None] * jnp.einsum('hsi,hij->hsj', key_f, later, precision=exact_arithmetic)
        sig = jax.nn.sigmoid(query_before_norm)
        query_pre_gradient = join_heads(d_query) * (sig * (1.0 + query_before_norm * (1.0 - sig)))
        value_flat_gradient = join_heads(d_value)
        low_product_float = low_product.astype(jnp.float32)
        up_products = jnp.stack([adapter_scale * jnp.dot(low_product_float[:, :ADAPTER_RANK].T, query_pre_gradient, precision=exact_arithmetic), adapter_scale * jnp.dot(low_product_float[:, ADAPTER_RANK:].T, value_flat_gradient, precision=exact_arithmetic)])
        low_gradient = adapter_scale * jnp.concatenate([jnp.dot(query_pre_gradient, lifting_matrices[0].astype(jnp.float32).T, precision=exact_arithmetic), jnp.dot(value_flat_gradient, lifting_matrices[1].astype(jnp.float32).T, precision=exact_arithmetic)], axis=1)
        down_terms = jnp.dot(input_rows.astype(jnp.float32).T, low_gradient, precision=exact_arithmetic)
        later_next = carried + gain[:, None, None] * later
        return ((later_next, grad_down + down_terms, grad_up + up_products), None)
    init = (zero_state, jnp.zeros((MODEL_WIDTH, 2 * ADAPTER_RANK), jnp.float32), jnp.zeros((2, ADAPTER_RANK, HEADS * HK), jnp.float32))
    (_, grad_down, grad_up), _ = lax.scan(backward_step, init, (blocks, states), reverse=True)
    return (grad_down, grad_up)
```

```python
import jax
import jax.numpy as jnp
from jax import lax
from jax.experimental import pallas as pl
from jax.experimental.pallas import tpu as pltpu
from jax.sharding import Mesh, PartitionSpec as P

bf16, f32 = jnp.bfloat16, jnp.float32
adapter_scale = 2.0
eps_norm = 1e-06
VMEM = pl.BlockSpec(memory_space=pltpu.VMEM)
SMEM = pl.BlockSpec(memory_space=pltpu.SMEM)
ANY = pl.BlockSpec(memory_space=pl.ANY)


def dot(a, b):
    return jnp.dot(a, b, preferred_element_type=f32)


def dot_t(a, b):
    return lax.dot_general(a, b, (((1,), (1,)), ((), ())), preferred_element_type=f32)


def t_dot(a, b):
    return lax.dot_general(a, b, (((0,), (0,)), ((), ())), preferred_element_type=f32)


def shape(dims, dtype=bf16):
    return jax.ShapeDtypeStruct(dims, dtype)


def call(kernel, outs, *args, mib=6, specs=None, scratch=()):
    return pl.pallas_call(
        kernel,
        out_shape=outs,
        in_specs=specs or [VMEM] * len(args),
        out_specs=jax.tree.map(lambda _: VMEM, outs),
        scratch_shapes=scratch,
        compiler_params=pltpu.CompilerParams(vmem_limit_bytes=mib << 20),
    )(*args)


def pack_kernel(a, b, c, grad, decay, out):
    d = decay[...]
    hi = d.astype(bf16).astype(f32)
    mid = (d - hi).astype(bf16).astype(f32)
    lo = (d - hi - mid).astype(bf16).astype(f32)
    zero = jnp.zeros((13, 128), f32)
    for h in range(out.shape[0]):
        lanes = slice(h * 128, h * 128 + 128)
        out[h, 0:48, 0:128] = grad[0:48, lanes]
        out[h, 0:48, 128:256] = grad[48:96, lanes]
        out[h, 0:32, 256:384] = grad[96:128, lanes]
        logs = jnp.concatenate([hi[h : h + 1], mid[h : h + 1], lo[h : h + 1], zero], axis=0)
        out[h, 32:48, 256:384] = logs.astype(bf16)
        for i, m in enumerate((a, b, c)):
            out[h, 48:, i * 128 : (i + 1) * 128] = m[:, lanes]


def project_kernel(ids, w_all, down, *rest):
    pieces, rest = rest[:10], rest[10:]
    lift, tail, extra, k_ref, v_ref, q_ref, qpre_ref, low_ref, tok, send_ref, wbuf, sems = rest
    ny, nz, deep, wide = wbuf.shape
    y, c = ids[0], ids[1]
    width = tok.shape[2]
    copies = []
    for i in range(ny):
        copies.append((w_all.at[:, i * deep : (i + 1) * deep, :], wbuf.at[i, :, :, : wide - 128]))
    copies.append((down, wbuf.at[:, :, :, wide - 128 :]))
    half = tok.shape[1] // 2
    for i, p in enumerate(pieces):
        rel = (0, 0, ny - 1, ny - 1, 1, 1, 2, 2, 2, 2)[i]
        core = c if i % 2 == 0 else 1 - c
        dst = tok.at[lax.rem(y + rel, ny) * 2 + core]
        if i >= 6:
            dst = dst.at[half * ((i - 6) // 2) : half * ((i - 6) // 2) + half]
        copies.append((p, dst))
    copies = [pltpu.make_async_copy(s, d, sems.at[i]) for i, (s, d) in enumerate(copies)]
    for copy in copies:
        copy.start()
    for i in range(ny + 1):
        copies[i].wait()
    send_ref[:, 96:112, :] = jnp.broadcast_to(extra[...][None], (send_ref.shape[0], 16, 128))
    for rel, used in ((0, (0, 1)), (ny - 1, (2, 3)), (1, (4, 5)), (2, (6, 7, 8, 9))):
        for i in used:
            copies[ny + 1 + i].wait()
        n = lax.rem(y + rel, ny)
        rows = pl.ds(pl.multiple_of(n * 256, 256), 256)
        x = tok[pl.ds(n * 2, 2)].reshape(256, width)
        w = wbuf[...].reshape(width, wide)
        acc = dot(x, w)
        low = acc[:, 384:].astype(bf16)
        low_ref[rows, :] = low
        u = acc[:, :128]
        k = (u * jax.nn.sigmoid(u)).astype(bf16)
        v = (acc[:, 128:256] + adapter_scale * dot(low, lift[1])).astype(bf16)
        u = acc[:, 256:384] + adapter_scale * dot(low, lift[0])
        k_ref[rows, :] = k
        v_ref[rows, :] = v
        qpre_ref[rows, :] = u
        q_ref[rows, :] = (u * jax.nn.sigmoid(u)).astype(bf16)
        faded = (k.astype(f32) * tail[rows, :]).astype(bf16)
        local = t_dot(faded, v).astype(bf16).reshape(-1, 16, 128)
        send_ref[:, pl.ds(pl.multiple_of(n * 16, 16), 16), :] = local
        side = t_dot(low, faded)[64:].reshape(-1, 8, 128)
        send_ref[:, pl.ds(pl.multiple_of(64 + n * 8, 8), 8), :] = side.astype(bf16)


def intra_kernel(q, k, v, dec, mixed, attn):
    for n in range(dec.shape[0]):
        rows = slice(n * 256, n * 256 + 256)
        m = (dot_t(q[rows, :], k[rows, :]) * dec[n]).astype(bf16)
        mixed[n] = m
        attn[rows, :] = dot(m, v[rows, :])


def scan_fwd_kernel(got, out, gains):
    nz, ny = got.shape[0], 4
    logs = got[:, 96:112, :].astype(f32)
    state = jnp.zeros((16, 128), f32)
    side = jnp.zeros((8, 128), f32)
    for y in range(ny):
        for z in range(nz):
            total = logs[z, 3 * y] + (logs[z, 3 * y + 1] + logs[z, 3 * y + 2])
            gain = jnp.exp(total)[None]
            gains[y * nz + z] = gain[0]
            out[z, 16 * y : 16 * y + 16, :] = state.astype(bf16)
            out[z, 64 + 8 * y : 72 + 8 * y, :] = side.astype(bf16)
            state = gain * state + got[z, 16 * y : 16 * y + 16, :].astype(f32)
            side = gain * side + got[z, 64 + 8 * y : 72 + 8 * y, :].astype(f32)


def scan_bwd_kernel(got, gains, out):
    nz, ny = got.shape[0], 4
    state = jnp.zeros((16, 128), f32)
    for y in reversed(range(ny)):
        for z in reversed(range(nz)):
            out[z, 16 * y : 16 * y + 16, :] = state.astype(bf16)
            state = gains[y * nz + z][None] * state + got[z, 16 * y : 16 * y + 16, :].astype(f32)
    up = jnp.sum(got[:, 64:80, :].astype(f32), axis=0).astype(bf16)
    out[:, 64:80, :] = jnp.broadcast_to(up[None], (nz, 16, 128))


def attn_kernel(q, k, v, qpre, low, mixed, attn_in, s_in, lead, bundle, dec, lift, send, dlow, dv):
    total_q = jnp.zeros((128, 128), f32)
    total_v = jnp.zeros((128, 128), f32)
    cross = jnp.zeros((64, 128), f32)
    for n in range(dec.shape[0]):
        rows = slice(n * 256, n * 256 + 256)
        s = s_in[:, n * 16 : n * 16 + 16, :].reshape(128, 128)
        side = s_in[:, 64 + n * 8 : 72 + n * 8, :].astype(f32).reshape(64, 128).astype(bf16)
        qn, vn, ln = q[rows, :], v[rows, :], low[rows, :]
        ahead = lead[rows, :]
        attn = attn_in[rows, :] + ahead * dot(qn, s)
        inv = lax.rsqrt(jnp.mean(attn * attn, axis=-1, keepdims=True) + eps_norm)
        normed = attn * inv
        parts = []
        for b in (2 * n, 2 * n + 1):
            parts += [bundle[b, 0:48, 0:128], bundle[b, 0:48, 128:256], bundle[b, 0:32, 256:384]]
        up = jnp.concatenate(parts, axis=0).astype(f32)
        d = (up - normed * jnp.mean(up * normed, axis=-1, keepdims=True)) * inv
        d = d.astype(bf16)
        carried = t_dot((qn.astype(f32) * ahead).astype(bf16), d).astype(bf16)
        send[:, n * 16 : n * 16 + 16, :] = carried.reshape(-1, 16, 128)
        cross += dot(side, carried)
        dm = (dot_t(d, vn) * dec[n]).astype(bf16)
        dq = dot(dm, k[rows, :]) + ahead * dot_t(d, s)
        u = qpre[rows, :]
        sig = jax.nn.sigmoid(u)
        dq = (dq * (sig * (1.0 + u * (1.0 - sig)))).astype(bf16)
        dlow[rows, :] = adapter_scale * dot_t(dq, lift[0])
        total_q += t_dot(ln, dq)
        dvn = t_dot(mixed[n], d)
        dv[rows, :] = dvn
        total_v += t_dot(ln, dvn.astype(bf16))
    up = adapter_scale * jnp.concatenate([total_q[:64], total_v[64:] + cross], axis=0)
    send[:, 64:80, :] = up.astype(bf16).reshape(-1, 16, 128)


def final_kernel(ids, dv, k, r_in, tail, lift, dlow_q, tok, keep, give, dlow, terms):
    for n in range(4):
        rows = slice(n * 256, n * 256 + 256)
        r = r_in[:, n * 16 : n * 16 + 16, :].reshape(128, 128)
        d = (dv[rows, :] + tail[rows, :] * dot(k[rows, :], r)).astype(bf16)
        dlow[rows, :] = (dlow_q[rows, :] + adapter_scale * dot_t(d, lift[1])).astype(bf16)
    small = dlow[...].astype(f32).T.astype(bf16)
    wide = 512
    tokens = tok.shape[0] * tok.shape[1]
    for m in range(0, tok.shape[2], wide):
        x = tok[:, :, m : m + wide].reshape(tokens, wide)
        terms[m : m + wide, :] = dot(small, x).T
    per = keep.shape[1] // 8
    first = ids[1] == 0
    for b in range(16):
        y, x = b // 4, b % 4
        halves = []
        for c in range(2):
            base = ((y * 16 + c) * 4 + x) * per
            rows = [terms[pl.ds(base + r, 8, stride=8 * per), :] for r in range(per)]
            halves.append(jnp.concatenate(rows, axis=0))
        keep[b] = jnp.where(first, halves[0], halves[1])
        give[b] = jnp.where(first, halves[1], halves[0]).astype(bf16)


def add_kernel(a, b, out):
    out[...] = (a[...] + b[...].astype(f32)).astype(bf16)


def fold_kernel(got, out, tmp):
    tmp[...] = jnp.sum(got[...].astype(f32), axis=0)
    nz = out.shape[0]
    per = tmp.shape[0] // nz
    for z in range(nz):
        out[z] = jnp.concatenate(
            [tmp[pl.ds(z, per, stride=nz), :], jnp.zeros((out.shape[1] - per, 128), f32)], axis=0
        ).astype(bf16)


def last_kernel(got, out):
    out[...] = jnp.sum(got[...].astype(f32), axis=0)[: out.shape[0]]


def up_kernel(ids, own, other, *rest):
    pieces, out = rest[:-1], rest[-1]
    y, c = ids[0], ids[1]

    def put(yy, cc, val):
        out[:, pl.ds(pl.multiple_of((yy * 2 + cc) * 128, 128), 128)] = val.astype(f32)

    put(y, c, own[...])
    put(y, 1 - c, other[...])
    for i, rel in enumerate((3, 1, 2)):
        yy = lax.rem(y + rel, 4)
        put(yy, c, pieces[i][0])
        put(yy, 1 - c, pieces[i][1])


def on_device(tokens, wq, wk, wv, down, lift, decay, grad):
    own, width = tokens.shape
    rank = lift.shape[1]
    heads = decay.shape[0]
    hk = wq.shape[1] // heads
    group = ("y", "c")
    ny, nz, nc, nx = (lax.axis_size(a) for a in ("y", "z", "c", "x"))
    ids = jnp.stack([lax.axis_index("y"), lax.axis_index("c")]).astype(jnp.int32)
    head = lax.axis_index("y") * nc + lax.axis_index("c")
    rows = wq.shape[0]
    span = nc * own
    count = ny * span
    ring = lambda v, s: lax.ppermute(v, "y", [(i, (i + s) % ny) for i in range(ny)])
    swap = lambda v: lax.ppermute(v, "c", [(0, 1), (1, 0)])

    below, above = ring(tokens, 1), ring(tokens, -1)
    far0, far1 = ring(below[: own // 2], 1), ring(above[own // 2 :], -1)
    pieces = []
    for p in (tokens, below, above, far0, far1):
        pieces += [p, swap(p)]

    bundle = call(
        pack_kernel, shape((heads, 48 + rows, 3 * hk)), wk, wv, wq, grad, decay
    )
    bundle = lax.all_to_all(bundle, group, 0, 0, tiled=True)
    w = bundle[:, 48:].reshape(heads * rows, 3 * hk)
    w = lax.all_gather(w, "z")

    logs = bundle[:, 32:35, 2 * hk :].astype(f32)
    logs = (logs[:, 0] + (logs[:, 1] + logs[:, 2])).reshape(ny, span)
    lift = lax.dynamic_slice_in_dim(lift, head * hk, hk, 2)
    zero = jnp.zeros((rank, hk), bf16)
    lift = jnp.stack([jnp.concatenate([lift[0], zero]), jnp.concatenate([zero, lift[1]])])
    cum = jnp.cumsum(logs, axis=1)
    total = cum[:, -1]
    wide = lambda a: jnp.broadcast_to(a.reshape(count, 1), (count, hk))
    lead = wide(jnp.exp(cum))
    tail = wide(jnp.exp(total[:, None] - cum))
    causal = (jnp.arange(span)[:, None] >= jnp.arange(span)[None, :])[None]
    dec = jnp.where(causal, jnp.exp(jnp.where(causal, cum[:, :, None] - cum[:, None, :], 0.0)), 0.0)
    extra = jnp.stack(split3(total), axis=1).reshape(3 * ny, 1)
    extra = jnp.broadcast_to(jnp.pad(extra, ((0, 16 - 3 * ny), (0, 0))), (16, hk))

    deep = nc * rows
    k, v, q, qpre, low, tok, send = call(
        project_kernel,
        (
            shape((count, hk)), shape((count, hk)), shape((count, hk)), shape((count, hk), f32),
            shape((count, hk)), shape((heads, own, width)), shape((nz, 112, hk)),
        ),
        ids, w, down.reshape(ny, nz, deep, 2 * rank), *pieces, lift, tail, extra,
        mib=20,
        specs=[SMEM] + [ANY] * 12 + [VMEM] * 3,
        scratch=[
            pltpu.VMEM((ny, nz, deep, 3 * hk + 2 * rank), bf16),
            pltpu.SemaphoreType.DMA((ny + 11,)),
        ],
    )

    got = lax.all_to_all(send, "z", 0, 0, tiled=True)
    mixed, attn_in = call(intra_kernel, (shape((ny, span, span)), shape((count, hk), f32)), q, k, v, dec)
    back, gains = call(scan_fwd_kernel, (shape((nz, 96, hk)), shape((nz * ny, hk), f32)), got)
    s_in = lax.all_to_all(back, "z", 0, 0, tiled=True)

    send, dlow_q, dv = call(
        attn_kernel,
        (shape((nz, 80, hk)), shape((count, 2 * rank), f32), shape((count, hk), f32)),
        q, k, v, qpre, low, mixed, attn_in, s_in, lead, bundle, dec, lift,
    )
    got = lax.all_to_all(send, "z", 0, 0, tiled=True)
    back = call(scan_bwd_kernel, shape((nz, 80, hk)), got, gains)
    r_in = lax.all_to_all(back, "z", 0, 0, tiled=True)

    up = r_in[:, 64:80].reshape(2 * rank, hk)
    up_other = swap(up)
    pair = jnp.stack([up, up_other])
    ups = [ring(pair, 1), ring(pair, -1), ring(pair, 2)]

    out_rows = width // (ny * nz * nc * nx)
    keep, give = call(
        final_kernel,
        (shape((ny * nx, nz * out_rows, hk), f32), shape((ny * nx, nz * out_rows, hk))),
        ids, dv, k, r_in, tail, lift, dlow_q, tok,
        specs=[SMEM] + [VMEM] * 7,
        scratch=[pltpu.VMEM((count, 2 * rank), bf16), pltpu.VMEM((width, 2 * rank), f32)],
        mib=12,
    )
    down_terms = call(add_kernel, shape(give.shape), keep, swap(give))
    down_terms = lax.all_to_all(down_terms, ("y", "x"), 0, 0, tiled=True)
    down_terms = call(
        fold_kernel, shape((nz, 16, hk)), down_terms,
        scratch=[pltpu.VMEM((nz * out_rows, hk), f32)],
    )
    down_terms = lax.all_to_all(down_terms, "z", 0, 0, tiled=True)
    grad_down = call(last_kernel, shape((out_rows, hk), f32), down_terms)
    grad_up = call(
        up_kernel, shape((2 * rank, heads * hk), f32), ids, up, up_other, *ups,
        specs=[SMEM] + [VMEM] * 5,
    )
    return (grad_down, grad_up.reshape(2, rank, heads * hk))


def split3(v):
    hi = lax.reduce_precision(v, 8, 7)
    mid = lax.reduce_precision(v - hi, 8, 7)
    lo = lax.reduce_precision(v - hi - mid, 8, 7)
    return hi.astype(bf16), mid.astype(bf16), lo.astype(bf16)


def solution(mesh):
    n_mp = mesh.shape["mp"]
    wide = Mesh(mesh.devices.reshape(4, 8, 2, n_mp), ("y", "z", "c", "x"))
    seq = ("y", "z", "c")
    return jax.shard_map(
        on_device,
        mesh=wide,
        in_specs=(
            P(seq, None),
            P(seq, "x"),
            P(seq, "x"),
            P(seq, "x"),
            P(),
            P(None, None, "x"),
            P("x", seq),
            P(seq, "x"),
        ),
        out_specs=(P(("y", "z", "c", "x"), None), P(None, None, "x")),
        check_vma=False,
    )
```

```python
import jax
import jax.numpy as jnp
from jax import lax
from jax.experimental import pallas as pl
from jax.experimental.pallas import tpu as pltpu
from jax.sharding import Mesh, PartitionSpec as P


bf16, f32 = jnp.bfloat16, jnp.float32
adapter_scale = 2.0
eps_norm = 1e-06
VMEM = pl.BlockSpec(memory_space=pltpu.VMEM)
SMEM = pl.BlockSpec(memory_space=pltpu.SMEM)
ANY = pl.BlockSpec(memory_space=pl.ANY)


def dot(a, b):
    return jnp.dot(a, b, preferred_element_type=f32)


def dot_t(a, b):
    return lax.dot_general(a, b, (((1,), (1,)), ((), ())), preferred_element_type=f32)


def t_dot(a, b):
    return lax.dot_general(a, b, (((0,), (0,)), ((), ())), preferred_element_type=f32)


def shape(dims, dtype=bf16):
    return jax.ShapeDtypeStruct(dims, dtype)


HBM = pl.BlockSpec(memory_space=pltpu.MemorySpace.HBM)


def call(kernel, outs, *args, mib=6, specs=None, out_specs=None, scratch=()):
    return pl.pallas_call(
        kernel,
        out_shape=outs,
        in_specs=specs or [VMEM] * len(args),
        out_specs=out_specs or jax.tree.map(lambda _: VMEM, outs),
        scratch_shapes=scratch,
        compiler_params=pltpu.CompilerParams(vmem_limit_bytes=mib << 20),
    )(*args)


def begin(pairs, sems, first=0):
    copies = [pltpu.make_async_copy(s, d, sems.at[first + i]) for i, (s, d) in enumerate(pairs)]
    for copy in copies:
        copy.start()
    return copies


def split3(d):
    hi = d.astype(bf16).astype(f32)
    mid = (d - hi).astype(bf16).astype(f32)
    return hi, mid, (d - hi - mid).astype(bf16).astype(f32)


def running(logs):
    n = logs.shape[1]
    t = lax.broadcasted_iota(jnp.int32, (n, n), 0)
    causal = lax.broadcasted_iota(jnp.int32, (n, n), 1) <= t
    terms = jnp.where(causal, jnp.broadcast_to(logs, (n, n)), 0.0)
    sums = jnp.dot(terms, jnp.ones((n, 128), f32), precision=lax.Precision.HIGHEST)
    return sums, causal


def pack_kernel(a_hbm, b_hbm, c_hbm, grad_hbm, decay_hbm, out, a, b, c, grad, decay, sems):
    src = (decay_hbm, grad_hbm, a_hbm, b_hbm, c_hbm)
    copies = begin(list(zip(src, (decay, grad, a, b, c))), sems)
    for copy in copies:
        copy.wait()
    hi, mid, lo = split3(decay[...])
    zero = jnp.zeros((13, 128), f32)
    for h in range(out.shape[0]):
        lanes = slice(h * 128, h * 128 + 128)
        out[h, 0:48, 0:128] = grad[0:48, lanes]
        out[h, 0:48, 128:256] = grad[48:96, lanes]
        out[h, 0:32, 256:384] = grad[96:128, lanes]
        logs = jnp.concatenate([hi[h : h + 1], mid[h : h + 1], lo[h : h + 1], zero], axis=0)
        out[h, 32:48, 256:384] = logs.astype(bf16)
        for i, m in enumerate((a, b, c)):
            out[h, 48:, i * 128 : (i + 1) * 128] = m[:, lanes]


def project_kernel(ids, down, *rest):
    weights, pieces, rest = rest[:9], rest[9:19], rest[19:]
    lift, logs, kvql_hbm, qpre_hbm, tok_hbm, send, wbuf, tok, kvql, qpre, tail, sems = rest
    ny, nz, _, wide = wbuf.shape
    y, c, z = ids[0], ids[1], ids[2]
    width = tok.shape[2]
    pairs = [(down, wbuf.at[:, :, :, wide - 128 :])]
    for i, p in enumerate(weights):
        shift = (0, -1, 1, -2, 2, -3, 3, 4, 4)[i]
        src = lax.rem(z + shift + nz, nz)
        span = (slice(0, ny), slice(0, ny // 2), slice(ny // 2, ny))[max(0, i - 6)]
        pairs.append((p, wbuf.at[span, src, :, : wide - 128]))
    half = tok.shape[1] // 2
    for i, p in enumerate(pieces):
        rel = (0, 0, ny - 1, ny - 1, 1, 1, 2, 2, 2, 2)[i]
        core = c if i % 2 == 0 else 1 - c
        dst = tok.at[lax.rem(y + rel, ny) * 2 + core]
        if i >= 6:
            dst = dst.at[half * ((i - 6) // 2) : half * ((i - 6) // 2) + half]
        pairs.append((p, dst))
    copies = begin(pairs, sems)
    ends = []
    for n in range(ny):
        sums, _ = running(logs[n : n + 1, :])
        total = sums[255:256, :]
        tail[n] = jnp.exp(total - sums)
        ends += list(split3(total))
    extra = jnp.concatenate(ends + [jnp.zeros((16 - len(ends), 128), f32)], axis=0).astype(bf16)
    send[:, 96:112, :] = jnp.broadcast_to(extra[None], (send.shape[0], 16, 128))
    for i in range(10):
        copies[i].wait()
    stores = []
    for step, (rel, used) in enumerate(
        ((0, (0, 1)), (ny - 1, (2, 3)), (1, (4, 5)), (2, (6, 7, 8, 9)))
    ):
        for i in used:
            copies[10 + i].wait()
        n = lax.rem(y + rel, ny)
        two = pl.ds(n * 2, 2)
        stores += begin([(tok.at[two], tok_hbm.at[two])], sems, 20 + 3 * step)
        acc = dot(tok[two].reshape(256, width), wbuf[...].reshape(width, wide))
        low = acc[:, 384:].astype(bf16)
        u = acc[:, :128]
        k = (u * jax.nn.sigmoid(u)).astype(bf16)
        v = (acc[:, 128:256] + adapter_scale * dot(low, lift[1])).astype(bf16)
        u = acc[:, 256:384] + adapter_scale * dot(low, lift[0])
        q = (u * jax.nn.sigmoid(u)).astype(bf16)
        faded = (k.astype(f32) * tail[n]).astype(bf16)
        local = t_dot(faded, v).astype(bf16).reshape(-1, 16, 128)
        send[:, pl.ds(pl.multiple_of(n * 16, 16), 16), :] = local
        side = t_dot(low, faded)[64:].reshape(-1, 8, 128)
        send[:, pl.ds(pl.multiple_of(64 + n * 8, 8), 8), :] = side.astype(bf16)
        for i, m in enumerate((k, v, q, low)):
            kvql[step, i] = m
        qpre[step] = u
        stores += begin(
            [(kvql.at[step], kvql_hbm.at[n]), (qpre.at[step], qpre_hbm.at[n])], sems, 21 + 3 * step
        )
    for copy in stores:
        copy.wait()


def scan_fwd_kernel(got, out, gains):
    nz, ny = got.shape[0], 4
    logs = got[:, 96:112, :].astype(f32)
    state = jnp.zeros((16, 128), f32)
    side = jnp.zeros((8, 128), f32)
    for y in range(ny):
        for z in range(nz):
            total = logs[z, 3 * y] + (logs[z, 3 * y + 1] + logs[z, 3 * y + 2])
            gain = jnp.exp(total)[None]
            gains[y * nz + z] = gain[0]
            out[z, 16 * y : 16 * y + 16, :] = state.astype(bf16)
            out[z, 64 + 8 * y : 72 + 8 * y, :] = side.astype(bf16)
            state = gain * state + got[z, 16 * y : 16 * y + 16, :].astype(f32)
            side = gain * side + got[z, 64 + 8 * y : 72 + 8 * y, :].astype(f32)


def scan_bwd_kernel(got, gains, out):
    nz, ny = got.shape[0], 4
    state = jnp.zeros((16, 128), f32)
    for y in reversed(range(ny)):
        for z in reversed(range(nz)):
            out[z, 16 * y : 16 * y + 16, :] = state.astype(bf16)
            state = gains[y * nz + z][None] * state + got[z, 16 * y : 16 * y + 16, :].astype(f32)
    up = jnp.sum(got[:, 64:80, :].astype(f32), axis=0).astype(bf16)
    out[:, 64:80, :] = jnp.broadcast_to(up[None], (nz, 16, 128))


def attn_kernel(s_in, lift, logs, kvql_hbm, qpre_hbm, bundle_hbm, send, back_hbm, kvql, qpre, bundle, back, sems):
    ny = kvql.shape[0]
    copies = []
    for n in range(ny):
        copies += begin(
            [
                (kvql_hbm.at[n], kvql.at[n]),
                (qpre_hbm.at[n], qpre.at[n]),
                (bundle_hbm.at[2 * n : 2 * n + 2, 0:48, :], bundle.at[2 * n : 2 * n + 2]),
            ],
            sems,
            3 * n,
        )
    total_q = jnp.zeros((128, 128), f32)
    total_v = jnp.zeros((128, 128), f32)
    cross = jnp.zeros((64, 128), f32)
    stores = []
    for n in range(ny):
        s = s_in[:, n * 16 : n * 16 + 16, :].reshape(128, 128)
        side = s_in[:, 64 + n * 8 : 72 + n * 8, :].astype(f32).reshape(64, 128).astype(bf16)
        sums, causal = running(logs[n : n + 1, :])
        ahead = jnp.exp(sums)
        spread = jnp.concatenate([sums, sums], axis=1) - sums.T[0:1, :]
        dec = jnp.where(causal, jnp.exp(jnp.where(causal, spread, 0.0)), 0.0)
        for copy in copies[3 * n : 3 * n + 3]:
            copy.wait()
        k, v, q, low = (kvql[n, i] for i in range(4))
        mixed = (dot_t(q, k) * dec).astype(bf16)
        attn = dot(mixed, v) + ahead * dot(q, s)
        inv = lax.rsqrt(jnp.mean(attn * attn, axis=-1, keepdims=True) + eps_norm)
        normed = attn * inv
        parts = []
        for b in (2 * n, 2 * n + 1):
            parts += [bundle[b, :, 0:128], bundle[b, :, 128:256], bundle[b, 0:32, 256:384]]
        up = jnp.concatenate(parts, axis=0).astype(f32)
        d = (up - normed * jnp.mean(up * normed, axis=-1, keepdims=True)) * inv
        d = d.astype(bf16)
        carried = t_dot((q.astype(f32) * ahead).astype(bf16), d).astype(bf16)
        send[:, n * 16 : n * 16 + 16, :] = carried.reshape(-1, 16, 128)
        cross += dot(side, carried)
        dm = (dot_t(d, v) * dec).astype(bf16)
        dq = dot(dm, k) + ahead * dot_t(d, s)
        u = qpre[n]
        sig = jax.nn.sigmoid(u)
        dq = (dq * (sig * (1.0 + u * (1.0 - sig)))).astype(bf16)
        total_q += t_dot(low, dq)
        dv = t_dot(mixed, d)
        total_v += t_dot(low, dv.astype(bf16))
        back[n, 0] = dv
        back[n, 1] = adapter_scale * dot_t(dq, lift[0])
        stores += begin([(back.at[n], back_hbm.at[n])], sems, 12 + n)
    up = adapter_scale * jnp.concatenate([total_q[:64], total_v[64:] + cross], axis=0)
    send[:, 64:80, :] = up.astype(bf16).reshape(-1, 16, 128)
    for copy in stores:
        copy.wait()


def final_kernel(ids, r_in, lift, logs, kvql_hbm, back_hbm, tok_hbm, keep, give, k, back, tok, dlow, terms, sems):
    ny = k.shape[0]
    wide = 512
    blocks = tok.shape[2] // wide
    copies = []
    for n in range(ny):
        copies += begin([(kvql_hbm.at[n, 0], k.at[n]), (back_hbm.at[n], back.at[n])], sems, 2 * n)
    lanes = [slice(m * wide, m * wide + wide) for m in range(blocks)]
    parts = begin([(tok_hbm.at[:, :, m], tok.at[:, :, m]) for m in lanes], sems, 2 * ny)
    for n in range(ny):
        rows = slice(n * 256, n * 256 + 256)
        sums, _ = running(logs[n : n + 1, :])
        tail = jnp.exp(sums[255:256, :] - sums)
        r = r_in[:, n * 16 : n * 16 + 16, :].reshape(128, 128)
        copies[2 * n].wait()
        copies[2 * n + 1].wait()
        d = (back[n, 0] + tail * dot(k[n], r)).astype(bf16)
        dlow[rows, :] = back[n, 1] + adapter_scale * dot_t(d, lift[1])
    small = dlow[...].T.astype(bf16)
    tokens = tok.shape[0] * tok.shape[1]
    for m, part in zip(lanes, parts):
        part.wait()
        terms[m, :] = dot(small, tok[:, :, m].reshape(tokens, wide)).T
    per = keep.shape[1] // 8
    first = ids[1] == 0
    for b in range(16):
        y, x = b // 4, b % 4
        halves = []
        for c in range(2):
            base = ((y * 16 + c) * 4 + x) * per
            rows = [terms[pl.ds(base + r, 8, stride=8 * per), :] for r in range(per)]
            halves.append(jnp.concatenate(rows, axis=0))
        keep[b] = jnp.where(first, halves[0], halves[1])
        give[b] = jnp.where(first, halves[1], halves[0]).astype(bf16)


def add_kernel(a, b, out):
    out[...] = (a[...] + b[...].astype(f32)).astype(bf16)


def fold_kernel(got, out, tmp):
    tmp[...] = jnp.sum(got[...].astype(f32), axis=0)
    nz = out.shape[0]
    per = tmp.shape[0] // nz
    for z in range(nz):
        out[z] = jnp.concatenate(
            [tmp[pl.ds(z, per, stride=nz), :], jnp.zeros((out.shape[1] - per, 128), f32)], axis=0
        ).astype(bf16)


def last_kernel(got, out):
    out[...] = jnp.sum(got[...].astype(f32), axis=0)[: out.shape[0]]


def up_kernel(ids, own, other, *rest):
    pieces, out = rest[:-1], rest[-1]
    y, c = ids[0], ids[1]

    def put(yy, cc, val):
        out[:, pl.ds(pl.multiple_of((yy * 2 + cc) * 128, 128), 128)] = val.astype(f32)

    put(y, c, own[...])
    put(y, 1 - c, other[...])
    for i, rel in enumerate((3, 1, 2)):
        yy = lax.rem(y + rel, 4)
        put(yy, c, pieces[i][0])
        put(yy, 1 - c, pieces[i][1])


def layer(tokens, wq, wk, wv, down, lift, decay, grad):
    own, width = tokens.shape
    rank = lift.shape[1]
    heads = decay.shape[0]
    hk = wq.shape[1] // heads
    group = ("y", "c")
    ny, nz, nc, nx = (lax.axis_size(a) for a in ("y", "z", "c", "x"))
    ids = jnp.stack([lax.axis_index(a) for a in ("y", "c", "z")]).astype(jnp.int32)
    head = lax.axis_index("y") * nc + lax.axis_index("c")
    rows = wq.shape[0]
    span = nc * own
    ring = lambda v, s, a="y", n=ny: lax.ppermute(v, a, [(i, (i + s) % n) for i in range(n)])
    swap = lambda v: lax.ppermute(v, "c", [(0, 1), (1, 0)])
    DMA = pltpu.SemaphoreType.DMA

    below = ring(tokens, 1)
    above = ring(tokens, -1)
    far0, far1 = ring(below[: own // 2], 1), ring(above[own // 2 :], -1)
    pieces = []
    for p in (tokens, below, above, far0, far1):
        pieces += [p, swap(p)]

    bundle = call(
        pack_kernel, shape((heads, 48 + rows, 3 * hk)), wk, wv, wq, grad, decay,
        specs=[HBM] * 5,
        mib=60,
        scratch=[pltpu.VMEM(wk.shape, bf16)] * 3
        + [pltpu.VMEM(grad.shape, bf16), pltpu.VMEM(decay.shape, f32), DMA((5,))],
    )
    bundle = lax.all_to_all(bundle, group, 0, 0, tiled=True)
    w = bundle[:, 48:].reshape(heads * rows, 3 * hk)
    weights, ahead, behind = [w], w, w
    for _ in range(nz // 2 - 1):
        ahead, behind = ring(ahead, 1, "z", nz), ring(behind, -1, "z", nz)
        weights += [ahead, behind]
    half = heads * rows // 2
    weights += [ring(ahead[:half], 1, "z", nz), ring(behind[half:], -1, "z", nz)]
    deep = nc * rows
    weights = [p.reshape(-1, deep, 3 * hk) for p in weights]

    logs = bundle[:, 32:35, 2 * hk :].astype(f32)
    logs = (logs[:, 0] + (logs[:, 1] + logs[:, 2])).reshape(ny, span)
    lift = lax.dynamic_slice_in_dim(lift, head * hk, hk, 2)
    zero = jnp.zeros((rank, hk), bf16)
    lift = jnp.stack([jnp.concatenate([lift[0], zero]), jnp.concatenate([zero, lift[1]])])

    kvql, qpre, tok, send = call(
        project_kernel,
        (
            shape((ny, 4, span, hk)), shape((ny, span, hk), f32),
            shape((heads, own, width)), shape((nz, 112, hk)),
        ),
        ids, down.reshape(ny, nz, deep, 2 * rank), *weights, *pieces, lift, logs,
        mib=60,
        specs=[SMEM] + [HBM] * 20 + [VMEM] * 2,
        out_specs=(HBM, HBM, HBM, VMEM),
        scratch=[
            pltpu.VMEM((ny, nz, deep, 3 * hk + 2 * rank), bf16),
            pltpu.VMEM((heads, own, width), bf16),
            pltpu.VMEM((ny, 4, span, hk), bf16),
            pltpu.VMEM((ny, span, hk), f32),
            pltpu.VMEM((ny, span, hk), f32),
            DMA((32,)),
        ],
    )

    got = lax.all_to_all(send, "z", 0, 0, tiled=True)
    scanned, gains = call(scan_fwd_kernel, (shape((nz, 96, hk)), shape((nz * ny, hk), f32)), got)
    s_in = lax.all_to_all(scanned, "z", 0, 0, tiled=True)

    send, back = call(
        attn_kernel,
        (shape((nz, 80, hk)), shape((ny, 2, span, hk), f32)),
        s_in, lift, logs, kvql, qpre, bundle,
        mib=60,
        specs=[VMEM] * 3 + [HBM] * 3,
        out_specs=(VMEM, HBM),
        scratch=[
            pltpu.VMEM((ny, 4, span, hk), bf16),
            pltpu.VMEM((ny, span, hk), f32),
            pltpu.VMEM((heads, 48, 3 * hk), bf16),
            pltpu.VMEM((ny, 2, span, hk), f32),
            DMA((16,)),
        ],
    )
    got = lax.all_to_all(send, "z", 0, 0, tiled=True)
    scanned = call(scan_bwd_kernel, shape((nz, 80, hk)), got, gains)
    r_in = lax.all_to_all(scanned, "z", 0, 0, tiled=True)

    up = r_in[:, 64:80].reshape(2 * rank, hk)
    up_other = swap(up)
    pair = jnp.stack([up, up_other])
    ups = [ring(pair, 1), ring(pair, -1), ring(pair, 2)]

    out_rows = width // (ny * nz * nc * nx)
    keep, give = call(
        final_kernel,
        (shape((ny * nx, nz * out_rows, hk), f32), shape((ny * nx, nz * out_rows, hk))),
        ids, r_in, lift, logs, kvql, back, tok,
        specs=[SMEM] + [VMEM] * 3 + [HBM] * 3,
        scratch=[
            pltpu.VMEM((ny, span, hk), bf16),
            pltpu.VMEM((ny, 2, span, hk), f32),
            pltpu.VMEM((heads, own, width), bf16),
            pltpu.VMEM((heads * own, 2 * rank), f32),
            pltpu.VMEM((width, 2 * rank), f32),
            DMA((16,)),
        ],
        mib=60,
    )
    down_terms = call(add_kernel, shape(give.shape), keep, swap(give))
    down_terms = lax.all_to_all(down_terms, ("y", "x"), 0, 0, tiled=True)
    down_terms = call(
        fold_kernel, shape((nz, 16, hk)), down_terms,
        scratch=[pltpu.VMEM((nz * out_rows, hk), f32)],
    )
    down_terms = lax.all_to_all(down_terms, "z", 0, 0, tiled=True)
    grad_down = call(last_kernel, shape((out_rows, hk), f32), down_terms)
    grad_up = call(
        up_kernel, shape((2 * rank, heads * hk), f32), ids, up, up_other, *ups,
        specs=[SMEM] + [VMEM] * 5,
    )
    return (grad_down, grad_up.reshape(2, rank, heads * hk))


def solution(mesh):
    n_mp = mesh.shape["mp"]
    wide = Mesh(mesh.devices.reshape(4, 8, 2, n_mp), ("y", "z", "c", "x"))
    seq = ("y", "z", "c")
    return jax.shard_map(
        layer,
        mesh=wide,
        in_specs=(
            P(seq, None),
            P(seq, "x"),
            P(seq, "x"),
            P(seq, "x"),
            P(),
            P(None, None, "x"),
            P("x", seq),
            P(seq, "x"),
        ),
        out_specs=(P(("y", "z", "c", "x"), None), P(None, None, "x")),
        check_vma=False,
    )
```

```python
import jax
import jax.numpy as jnp
from jax import lax
from jax.experimental import pallas as pl
from jax.experimental.pallas import tpu as pltpu
from jax.sharding import Mesh, PartitionSpec as P


bf16, f32 = jnp.bfloat16, jnp.float32
adapter_scale = 2.0
eps_norm = 1e-06
VMEM = pl.BlockSpec(memory_space=pltpu.VMEM)
SMEM = pl.BlockSpec(memory_space=pltpu.SMEM)
ANY = pl.BlockSpec(memory_space=pl.ANY)


def dot(a, b):
    return jnp.dot(a, b, preferred_element_type=f32)


def dot_t(a, b):
    return lax.dot_general(a, b, (((1,), (1,)), ((), ())), preferred_element_type=f32)


def t_dot(a, b):
    return lax.dot_general(a, b, (((0,), (0,)), ((), ())), preferred_element_type=f32)


def shape(dims, dtype=bf16):
    return jax.ShapeDtypeStruct(dims, dtype)


HBM = pl.BlockSpec(memory_space=pltpu.MemorySpace.HBM)


def call(kernel, outs, *args, mib=6, specs=None, out_specs=None, scratch=()):
    return pl.pallas_call(
        kernel,
        out_shape=outs,
        in_specs=specs or [VMEM] * len(args),
        out_specs=out_specs or jax.tree.map(lambda _: VMEM, outs),
        scratch_shapes=scratch,
        compiler_params=pltpu.CompilerParams(vmem_limit_bytes=mib << 20),
    )(*args)


def begin(pairs, sems, first=0):
    copies = [pltpu.make_async_copy(s, d, sems.at[first + i]) for i, (s, d) in enumerate(pairs)]
    for copy in copies:
        copy.start()
    return copies


def split3(d):
    hi = d.astype(bf16).astype(f32)
    mid = (d - hi).astype(bf16).astype(f32)
    return hi, mid, (d - hi - mid).astype(bf16).astype(f32)


def running(logs):
    chunks, n = logs.shape
    parts = jnp.concatenate(list(split3(logs)) + [jnp.zeros((16 - 3 * chunks, n), f32)], axis=0)
    ones = lax.broadcasted_iota(jnp.int32, (n, n), 0) <= lax.broadcasted_iota(jnp.int32, (n, n), 1)
    sums = dot(parts.astype(bf16), ones.astype(f32).astype(bf16))
    return sums[:chunks] + (sums[chunks : 2 * chunks] + sums[2 * chunks : 3 * chunks])


def down_rows(row):
    return jnp.broadcast_to(row, (128, row.shape[1])).T


def pack_kernel(a_hbm, b_hbm, c_hbm, grad_hbm, decay_hbm, out, a, b, c, grad, decay, sems):
    src = (decay_hbm, grad_hbm, a_hbm, b_hbm, c_hbm)
    copies = begin(list(zip(src, (decay, grad, a, b, c))), sems)
    for copy in copies:
        copy.wait()
    hi, mid, lo = split3(decay[...])
    zero = jnp.zeros((13, 128), f32)
    for h in range(out.shape[0]):
        lanes = slice(h * 128, h * 128 + 128)
        out[h, 0:48, 0:128] = grad[0:48, lanes]
        out[h, 0:48, 128:256] = grad[48:96, lanes]
        out[h, 0:32, 256:384] = grad[96:128, lanes]
        logs = jnp.concatenate([hi[h : h + 1], mid[h : h + 1], lo[h : h + 1], zero], axis=0)
        out[h, 32:48, 256:384] = logs.astype(bf16)
        for i, m in enumerate((a, b, c)):
            out[h, 48:, i * 128 : (i + 1) * 128] = m[:, lanes]


def project_kernel(ids, down, *rest):
    weights, pieces, rest = rest[:9], rest[9:19], rest[19:]
    lift, logs, kvql_hbm, qpre_hbm, tok_hbm, send, wbuf, tok, kvql, qpre, tail, sems = rest
    ny, nz, _, wide = wbuf.shape
    y, c, z = ids[0], ids[1], ids[2]
    width = tok.shape[2]
    pairs = [(down, wbuf.at[:, :, :, wide - 128 :])]
    for i, p in enumerate(weights):
        shift = (0, -1, 1, -2, 2, -3, 3, 4, 4)[i]
        src = lax.rem(z + shift + nz, nz)
        span = (slice(0, ny), slice(0, ny // 2), slice(ny // 2, ny))[max(0, i - 6)]
        pairs.append((p, wbuf.at[span, src, :, : wide - 128]))
    half = tok.shape[1] // 2
    for i, p in enumerate(pieces):
        rel = (0, 0, ny - 1, ny - 1, 1, 1, 2, 2, 2, 2)[i]
        core = c if i % 2 == 0 else 1 - c
        dst = tok.at[lax.rem(y + rel, ny) * 2 + core]
        if i >= 6:
            dst = dst.at[half * ((i - 6) // 2) : half * ((i - 6) // 2) + half]
        pairs.append((p, dst))
    copies = begin(pairs, sems)
    ends = []
    cum = running(logs[...])
    for n in range(ny):
        sums = down_rows(cum[n : n + 1, :])
        total = sums[255:256, :]
        tail[n] = jnp.exp(total - sums)
        ends += list(split3(total))
    extra = jnp.concatenate(ends + [jnp.zeros((16 - len(ends), 128), f32)], axis=0).astype(bf16)
    send[:, 96:112, :] = jnp.broadcast_to(extra[None], (send.shape[0], 16, 128))
    for i in range(10):
        copies[i].wait()
    stores = []
    for step, (rel, used) in enumerate(
        ((0, (0, 1)), (ny - 1, (2, 3)), (1, (4, 5)), (2, (6, 7, 8, 9)))
    ):
        for i in used:
            copies[10 + i].wait()
        n = lax.rem(y + rel, ny)
        two = pl.ds(n * 2, 2)
        stores += begin([(tok.at[two], tok_hbm.at[two])], sems, 20 + 3 * step)
        acc = dot(tok[two].reshape(256, width), wbuf[...].reshape(width, wide))
        low = acc[:, 384:].astype(bf16)
        u = acc[:, :128]
        k = (u * jax.nn.sigmoid(u)).astype(bf16)
        v = (acc[:, 128:256] + adapter_scale * dot(low, lift[1])).astype(bf16)
        u = acc[:, 256:384] + adapter_scale * dot(low, lift[0])
        q = (u * jax.nn.sigmoid(u)).astype(bf16)
        faded = (k.astype(f32) * tail[n]).astype(bf16)
        local = t_dot(faded, v).astype(bf16).reshape(-1, 16, 128)
        send[:, pl.ds(pl.multiple_of(n * 16, 16), 16), :] = local
        side = t_dot(low, faded)[64:].reshape(-1, 8, 128)
        send[:, pl.ds(pl.multiple_of(64 + n * 8, 8), 8), :] = side.astype(bf16)
        for i, m in enumerate((k, v, q, low)):
            kvql[step, i] = m
        qpre[step] = u
        stores += begin(
            [(kvql.at[step], kvql_hbm.at[n]), (qpre.at[step], qpre_hbm.at[n])], sems, 21 + 3 * step
        )
    for copy in stores:
        copy.wait()


def scan_fwd_kernel(got, out, gains):
    nz, ny = got.shape[0], 4
    logs = got[:, 96:112, :].astype(f32)
    state = jnp.zeros((16, 128), f32)
    side = jnp.zeros((8, 128), f32)
    for y in range(ny):
        for z in range(nz):
            total = logs[z, 3 * y] + (logs[z, 3 * y + 1] + logs[z, 3 * y + 2])
            gain = jnp.exp(total)[None]
            gains[y * nz + z] = gain[0]
            out[z, 16 * y : 16 * y + 16, :] = state.astype(bf16)
            out[z, 64 + 8 * y : 72 + 8 * y, :] = side.astype(bf16)
            state = gain * state + got[z, 16 * y : 16 * y + 16, :].astype(f32)
            side = gain * side + got[z, 64 + 8 * y : 72 + 8 * y, :].astype(f32)


def scan_bwd_kernel(got, gains, out):
    nz, ny = got.shape[0], 4
    state = jnp.zeros((16, 128), f32)
    for y in reversed(range(ny)):
        for z in reversed(range(nz)):
            out[z, 16 * y : 16 * y + 16, :] = state.astype(bf16)
            state = gains[y * nz + z][None] * state + got[z, 16 * y : 16 * y + 16, :].astype(f32)
    up = jnp.sum(got[:, 64:80, :].astype(f32), axis=0).astype(bf16)
    out[:, 64:80, :] = jnp.broadcast_to(up[None], (nz, 16, 128))


def attn_kernel(s_in, lift, logs, kvql_hbm, qpre_hbm, bundle_hbm, send, back_hbm, kvql, qpre, bundle, back, sems):
    ny = kvql.shape[0]
    copies = []
    for n in range(ny):
        copies += begin(
            [
                (kvql_hbm.at[n], kvql.at[n]),
                (qpre_hbm.at[n], qpre.at[n]),
                (bundle_hbm.at[2 * n : 2 * n + 2, 0:48, :], bundle.at[2 * n : 2 * n + 2]),
            ],
            sems,
            3 * n,
        )
    total_q = jnp.zeros((128, 128), f32)
    total_v = jnp.zeros((128, 128), f32)
    cross = jnp.zeros((64, 128), f32)
    stores = []
    cum = running(logs[...])
    square = (cum.shape[1], cum.shape[1])
    causal = lax.broadcasted_iota(jnp.int32, square, 1) <= lax.broadcasted_iota(jnp.int32, square, 0)
    for n in range(ny):
        s = s_in[:, n * 16 : n * 16 + 16, :].reshape(128, 128)
        side = s_in[:, 64 + n * 8 : 72 + n * 8, :].astype(f32).reshape(64, 128).astype(bf16)
        sums = down_rows(cum[n : n + 1, :])
        ahead = jnp.exp(sums)
        spread = jnp.concatenate([sums, sums], axis=1) - cum[n : n + 1, :]
        dec = jnp.where(causal, jnp.exp(jnp.where(causal, spread, 0.0)), 0.0)
        for copy in copies[3 * n : 3 * n + 3]:
            copy.wait()
        k, v, q, low = (kvql[n, i] for i in range(4))
        mixed = (dot_t(q, k) * dec).astype(bf16)
        attn = dot(mixed, v) + ahead * dot(q, s)
        inv = lax.rsqrt(jnp.mean(attn * attn, axis=-1, keepdims=True) + eps_norm)
        normed = attn * inv
        parts = []
        for b in (2 * n, 2 * n + 1):
            parts += [bundle[b, :, 0:128], bundle[b, :, 128:256], bundle[b, 0:32, 256:384]]
        up = jnp.concatenate(parts, axis=0).astype(f32)
        d = (up - normed * jnp.mean(up * normed, axis=-1, keepdims=True)) * inv
        d = d.astype(bf16)
        carried = t_dot((q.astype(f32) * ahead).astype(bf16), d).astype(bf16)
        send[:, n * 16 : n * 16 + 16, :] = carried.reshape(-1, 16, 128)
        cross += dot(side, carried)
        dm = (dot_t(d, v) * dec).astype(bf16)
        dq = dot(dm, k) + ahead * dot_t(d, s)
        u = qpre[n]
        sig = jax.nn.sigmoid(u)
        dq = (dq * (sig * (1.0 + u * (1.0 - sig)))).astype(bf16)
        total_q += t_dot(low, dq)
        dv = t_dot(mixed, d)
        total_v += t_dot(low, dv.astype(bf16))
        back[n, 0] = dv
        back[n, 1] = adapter_scale * dot_t(dq, lift[0])
        stores += begin([(back.at[n], back_hbm.at[n])], sems, 12 + n)
    up = adapter_scale * jnp.concatenate([total_q[:64], total_v[64:] + cross], axis=0)
    send[:, 64:80, :] = up.astype(bf16).reshape(-1, 16, 128)
    for copy in stores:
        copy.wait()


def final_kernel(ids, r_in, lift, logs, kvql_hbm, back_hbm, tok_hbm, keep, give, k, back, tok, dlow, terms, sems):
    ny = k.shape[0]
    wide = 512
    blocks = tok.shape[2] // wide
    copies = []
    for n in range(ny):
        copies += begin([(kvql_hbm.at[n, 0], k.at[n]), (back_hbm.at[n], back.at[n])], sems, 2 * n)
    lanes = [slice(m * wide, m * wide + wide) for m in range(blocks)]
    parts = begin([(tok_hbm.at[:, :, m], tok.at[:, :, m]) for m in lanes], sems, 2 * ny)
    cum = running(logs[...])
    for n in range(ny):
        rows = slice(n * 256, n * 256 + 256)
        sums = down_rows(cum[n : n + 1, :])
        tail = jnp.exp(sums[255:256, :] - sums)
        r = r_in[:, n * 16 : n * 16 + 16, :].reshape(128, 128)
        copies[2 * n].wait()
        copies[2 * n + 1].wait()
        d = (back[n, 0] + tail * dot(k[n], r)).astype(bf16)
        dlow[rows, :] = back[n, 1] + adapter_scale * dot_t(d, lift[1])
    small = dlow[...].T.astype(bf16)
    tokens = tok.shape[0] * tok.shape[1]
    for m, part in zip(lanes, parts):
        part.wait()
        terms[m, :] = dot(small, tok[:, :, m].reshape(tokens, wide)).T
    per = keep.shape[1] // 8
    first = ids[1] == 0
    for b in range(16):
        y, x = b // 4, b % 4
        halves = []
        for c in range(2):
            base = ((y * 16 + c) * 4 + x) * per
            rows = [terms[pl.ds(base + r, 8, stride=8 * per), :] for r in range(per)]
            halves.append(jnp.concatenate(rows, axis=0))
        keep[b] = jnp.where(first, halves[0], halves[1])
        give[b] = jnp.where(first, halves[1], halves[0]).astype(bf16)


def add_kernel(a, b, out):
    out[...] = (a[...] + b[...].astype(f32)).astype(bf16)


def fold_kernel(got, out, tmp):
    tmp[...] = jnp.sum(got[...].astype(f32), axis=0)
    nz = out.shape[0]
    per = tmp.shape[0] // nz
    for z in range(nz):
        out[z] = jnp.concatenate(
            [tmp[pl.ds(z, per, stride=nz), :], jnp.zeros((out.shape[1] - per, 128), f32)], axis=0
        ).astype(bf16)


def last_kernel(got, out):
    out[...] = jnp.sum(got[...].astype(f32), axis=0)[: out.shape[0]]


def up_kernel(ids, own, other, *rest):
    pieces, out = rest[:-1], rest[-1]
    y, c = ids[0], ids[1]

    def put(yy, cc, val):
        out[:, pl.ds(pl.multiple_of((yy * 2 + cc) * 128, 128), 128)] = val.astype(f32)

    put(y, c, own[...])
    put(y, 1 - c, other[...])
    for i, rel in enumerate((3, 1, 2)):
        yy = lax.rem(y + rel, 4)
        put(yy, c, pieces[i][0])
        put(yy, 1 - c, pieces[i][1])


def layer(tokens, wq, wk, wv, down, lift, decay, grad):
    own, width = tokens.shape
    rank = lift.shape[1]
    heads = decay.shape[0]
    hk = wq.shape[1] // heads
    group = ("y", "c")
    ny, nz, nc, nx = (lax.axis_size(a) for a in ("y", "z", "c", "x"))
    ids = jnp.stack([lax.axis_index(a) for a in ("y", "c", "z")]).astype(jnp.int32)
    head = lax.axis_index("y") * nc + lax.axis_index("c")
    rows = wq.shape[0]
    span = nc * own
    ring = lambda v, s, a="y", n=ny: lax.ppermute(v, a, [(i, (i + s) % n) for i in range(n)])
    swap = lambda v: lax.ppermute(v, "c", [(0, 1), (1, 0)])
    DMA = pltpu.SemaphoreType.DMA

    below = ring(tokens, 1)
    above = ring(tokens, -1)
    far0 = ring(below[: own // 2], 1)
    far1 = ring(above[own // 2 :], -1)
    pieces = []
    for p in (tokens, below, above, far0, far1):
        pieces += [p, swap(p)]

    bundle = call(
        pack_kernel, shape((heads, 48 + rows, 3 * hk)), wk, wv, wq, grad, decay,
        specs=[HBM] * 5,
        mib=60,
        scratch=[pltpu.VMEM(wk.shape, bf16)] * 3
        + [pltpu.VMEM(grad.shape, bf16), pltpu.VMEM(decay.shape, f32), DMA((5,))],
    )
    bundle = lax.all_to_all(bundle, group, 0, 0, tiled=True)
    w = bundle[:, 48:].reshape(heads * rows, 3 * hk)
    weights, ahead, behind = [w], w, w
    for _ in range(nz // 2 - 1):
        ahead = ring(ahead, 1, "z", nz)
        behind = ring(behind, -1, "z", nz)
        weights += [ahead, behind]
    half = heads * rows // 2
    weights.append(ring(ahead[:half], 1, "z", nz))
    weights.append(ring(behind[half:], -1, "z", nz))
    deep = nc * rows
    weights = [p.reshape(-1, deep, 3 * hk) for p in weights]

    logs = bundle[:, 32:35, 2 * hk :].astype(f32)
    logs = (logs[:, 0] + (logs[:, 1] + logs[:, 2])).reshape(ny, span)
    lift = lax.dynamic_slice_in_dim(lift, head * hk, hk, 2)
    zero = jnp.zeros((rank, hk), bf16)
    lift = jnp.stack([jnp.concatenate([lift[0], zero]), jnp.concatenate([zero, lift[1]])])

    kvql, qpre, tok, send = call(
        project_kernel,
        (
            shape((ny, 4, span, hk)), shape((ny, span, hk), f32),
            shape((heads, own, width)), shape((nz, 112, hk)),
        ),
        ids, down.reshape(ny, nz, deep, 2 * rank), *weights, *pieces, lift, logs,
        mib=60,
        specs=[SMEM] + [HBM] * 20 + [VMEM] * 2,
        out_specs=(HBM, HBM, HBM, VMEM),
        scratch=[
            pltpu.VMEM((ny, nz, deep, 3 * hk + 2 * rank), bf16),
            pltpu.VMEM((heads, own, width), bf16),
            pltpu.VMEM((ny, 4, span, hk), bf16),
            pltpu.VMEM((ny, span, hk), f32),
            pltpu.VMEM((ny, span, hk), f32),
            DMA((32,)),
        ],
    )

    got = lax.all_to_all(send, "z", 0, 0, tiled=True)
    scanned, gains = call(scan_fwd_kernel, (shape((nz, 96, hk)), shape((nz * ny, hk), f32)), got)
    s_in = lax.all_to_all(scanned, "z", 0, 0, tiled=True)

    send, back = call(
        attn_kernel,
        (shape((nz, 80, hk)), shape((ny, 2, span, hk), f32)),
        s_in, lift, logs, kvql, qpre, bundle,
        mib=60,
        specs=[VMEM] * 3 + [HBM] * 3,
        out_specs=(VMEM, HBM),
        scratch=[
            pltpu.VMEM((ny, 4, span, hk), bf16),
            pltpu.VMEM((ny, span, hk), f32),
            pltpu.VMEM((heads, 48, 3 * hk), bf16),
            pltpu.VMEM((ny, 2, span, hk), f32),
            DMA((16,)),
        ],
    )
    got = lax.all_to_all(send, "z", 0, 0, tiled=True)
    scanned = call(scan_bwd_kernel, shape((nz, 80, hk)), got, gains)
    r_in = lax.all_to_all(scanned, "z", 0, 0, tiled=True)

    up = r_in[:, 64:80].reshape(2 * rank, hk)
    up_other = swap(up)
    pair = jnp.stack([up, up_other])
    ups = [ring(pair, 1), ring(pair, -1), ring(pair, 2)]

    out_rows = width // (ny * nz * nc * nx)
    keep, give = call(
        final_kernel,
        (shape((ny * nx, nz * out_rows, hk), f32), shape((ny * nx, nz * out_rows, hk))),
        ids, r_in, lift, logs, kvql, back, tok,
        specs=[SMEM] + [VMEM] * 3 + [HBM] * 3,
        scratch=[
            pltpu.VMEM((ny, span, hk), bf16),
            pltpu.VMEM((ny, 2, span, hk), f32),
            pltpu.VMEM((heads, own, width), bf16),
            pltpu.VMEM((heads * own, 2 * rank), f32),
            pltpu.VMEM((width, 2 * rank), f32),
            DMA((16,)),
        ],
        mib=60,
    )
    down_terms = call(add_kernel, shape(give.shape), keep, swap(give))
    down_terms = lax.all_to_all(down_terms, ("y", "x"), 0, 0, tiled=True)
    down_terms = call(
        fold_kernel, shape((nz, 16, hk)), down_terms,
        scratch=[pltpu.VMEM((nz * out_rows, hk), f32)],
    )
    down_terms = lax.all_to_all(down_terms, "z", 0, 0, tiled=True)
    grad_down = call(last_kernel, shape((out_rows, hk), f32), down_terms)
    grad_up = call(
        up_kernel, shape((2 * rank, heads * hk), f32), ids, up, up_other, *ups,
        specs=[SMEM] + [VMEM] * 5,
    )
    return (grad_down, grad_up.reshape(2, rank, heads * hk))


def solution(mesh):
    n_mp = mesh.shape["mp"]
    wide = Mesh(mesh.devices.reshape(4, 8, 2, n_mp), ("y", "z", "c", "x"))
    seq = ("y", "z", "c")
    return jax.shard_map(
        layer,
        mesh=wide,
        in_specs=(
            P(seq, None),
            P(seq, "x"),
            P(seq, "x"),
            P(seq, "x"),
            P(),
            P(None, None, "x"),
            P("x", seq),
            P(seq, "x"),
        ),
        out_specs=(P(("y", "z", "c", "x"), None), P(None, None, "x")),
        check_vma=False,
    )
```

```python
import jax
import jax.numpy as jnp
from jax import lax
from jax.experimental import pallas as pl
from jax.experimental.pallas import tpu as pltpu
from jax.sharding import Mesh, PartitionSpec as P


bf16, f32 = jnp.bfloat16, jnp.float32
adapter_scale = 2.0
eps_norm = 1e-06
VMEM = pl.BlockSpec(memory_space=pltpu.VMEM)
SMEM = pl.BlockSpec(memory_space=pltpu.SMEM)
ANY = pl.BlockSpec(memory_space=pl.ANY)


def dot(a, b):
    return jnp.dot(a, b, preferred_element_type=f32)


def dot_t(a, b):
    return lax.dot_general(a, b, (((1,), (1,)), ((), ())), preferred_element_type=f32)


def t_dot(a, b):
    return lax.dot_general(a, b, (((0,), (0,)), ((), ())), preferred_element_type=f32)


def shape(dims, dtype=bf16):
    return jax.ShapeDtypeStruct(dims, dtype)


HBM = pl.BlockSpec(memory_space=pltpu.MemorySpace.HBM)


def call(kernel, outs, *args, mib=6, specs=None, out_specs=None, scratch=()):
    return pl.pallas_call(
        kernel,
        out_shape=outs,
        in_specs=specs or [VMEM] * len(args),
        out_specs=out_specs or jax.tree.map(lambda _: VMEM, outs),
        scratch_shapes=scratch,
        compiler_params=pltpu.CompilerParams(vmem_limit_bytes=mib << 20),
    )(*args)


def begin(pairs, sems, first=0):
    copies = [pltpu.make_async_copy(s, d, sems.at[first + i]) for i, (s, d) in enumerate(pairs)]
    for copy in copies:
        copy.start()
    return copies


def split3(d):
    hi = d.astype(bf16).astype(f32)
    mid = (d - hi).astype(bf16).astype(f32)
    return hi, mid, (d - hi - mid).astype(bf16).astype(f32)


def running(logs):
    chunks, n = logs.shape
    parts = jnp.concatenate(list(split3(logs)) + [jnp.zeros((16 - 3 * chunks, n), f32)], axis=0)
    ones = lax.broadcasted_iota(jnp.int32, (n, n), 0) <= lax.broadcasted_iota(jnp.int32, (n, n), 1)
    sums = dot(parts.astype(bf16), ones.astype(f32).astype(bf16))
    return sums[:chunks] + (sums[chunks : 2 * chunks] + sums[2 * chunks : 3 * chunks])


def down_rows(row):
    return jnp.broadcast_to(row, (128, row.shape[1])).T


def pack_kernel(a_hbm, b_hbm, c_hbm, grad_hbm, decay_hbm, out, a, b, c, grad, decay, sems):
    src = (decay_hbm, grad_hbm, a_hbm, b_hbm, c_hbm)
    copies = begin(list(zip(src, (decay, grad, a, b, c))), sems)
    for copy in copies:
        copy.wait()
    hi, mid, lo = split3(decay[...])
    zero = jnp.zeros((13, 128), f32)
    for h in range(out.shape[0]):
        lanes = slice(h * 128, h * 128 + 128)
        out[h, 0:48, 0:128] = grad[0:48, lanes]
        out[h, 0:48, 128:256] = grad[48:96, lanes]
        out[h, 0:32, 256:384] = grad[96:128, lanes]
        logs = jnp.concatenate([hi[h : h + 1], mid[h : h + 1], lo[h : h + 1], zero], axis=0)
        out[h, 32:48, 256:384] = logs.astype(bf16)
        for i, m in enumerate((a, b, c)):
            out[h, 48:, i * 128 : (i + 1) * 128] = m[:, lanes]


def project_kernel(ids, down, *rest):
    weights, pieces, rest = rest[:9], rest[9:19], rest[19:]
    lift, logs, kvql_hbm, qpre_hbm, tok_hbm, send, wbuf, tok, kvql, qpre, tail, sems = rest
    ny, nz, _, wide = wbuf.shape
    y, c, z = ids[0], ids[1], ids[2]
    width = tok.shape[2]
    pairs = [(down, wbuf.at[:, :, :, wide - 128 :])]
    for i, p in enumerate(weights):
        shift = (0, -1, 1, -2, 2, -3, 3, 4, 4)[i]
        src = lax.rem(z + shift + nz, nz)
        span = (slice(0, ny), slice(0, ny // 2), slice(ny // 2, ny))[max(0, i - 6)]
        pairs.append((p, wbuf.at[span, src, :, : wide - 128]))
    half = tok.shape[1] // 2
    for i, p in enumerate(pieces):
        rel = (0, 0, ny - 1, ny - 1, 1, 1, 2, 2, 2, 2)[i]
        core = c if i % 2 == 0 else 1 - c
        dst = tok.at[lax.rem(y + rel, ny) * 2 + core]
        if i >= 6:
            dst = dst.at[half * ((i - 6) // 2) : half * ((i - 6) // 2) + half]
        pairs.append((p, dst))
    copies = begin(pairs, sems)
    ends = []
    cum = running(logs[...])
    for n in range(ny):
        sums = down_rows(cum[n : n + 1, :])
        total = sums[255:256, :]
        tail[n] = jnp.exp(total - sums)
        ends += list(split3(total))
    extra = jnp.concatenate(ends + [jnp.zeros((16 - len(ends), 128), f32)], axis=0).astype(bf16)
    send[:, 96:112, :] = jnp.broadcast_to(extra[None], (send.shape[0], 16, 128))
    for i in range(10):
        copies[i].wait()
    stores = []
    for step, (rel, used) in enumerate(
        ((0, (0, 1)), (ny - 1, (2, 3)), (1, (4, 5)), (2, (6, 7, 8, 9)))
    ):
        for i in used:
            copies[10 + i].wait()
        n = lax.rem(y + rel, ny)
        two = pl.ds(n * 2, 2)
        stores += begin([(tok.at[two], tok_hbm.at[two])], sems, 20 + 3 * step)
        acc = dot(tok[two].reshape(256, width), wbuf[...].reshape(width, wide))
        low = acc[:, 384:].astype(bf16)
        u = acc[:, :128]
        k = (u * jax.nn.sigmoid(u)).astype(bf16)
        v = (acc[:, 128:256] + adapter_scale * dot(low, lift[1])).astype(bf16)
        u = acc[:, 256:384] + adapter_scale * dot(low, lift[0])
        q = (u * jax.nn.sigmoid(u)).astype(bf16)
        faded = (k.astype(f32) * tail[n]).astype(bf16)
        local = t_dot(faded, v).astype(bf16).reshape(-1, 16, 128)
        send[:, pl.ds(pl.multiple_of(n * 16, 16), 16), :] = local
        side = t_dot(low, faded)[64:].reshape(-1, 8, 128)
        send[:, pl.ds(pl.multiple_of(64 + n * 8, 8), 8), :] = side.astype(bf16)
        for i, m in enumerate((k, v, q, low)):
            kvql[step, i] = m
        qpre[step] = u
        stores += begin(
            [(kvql.at[step], kvql_hbm.at[n]), (qpre.at[step], qpre_hbm.at[n])], sems, 21 + 3 * step
        )
    for copy in stores:
        copy.wait()


def scan_fwd_kernel(got, out, gains):
    nz, ny = got.shape[0], 4
    logs = got[:, 96:112, :].astype(f32)
    state = jnp.zeros((16, 128), f32)
    side = jnp.zeros((8, 128), f32)
    for y in range(ny):
        for z in range(nz):
            total = logs[z, 3 * y] + (logs[z, 3 * y + 1] + logs[z, 3 * y + 2])
            gain = jnp.exp(total)[None]
            gains[y * nz + z] = gain[0]
            out[z, 16 * y : 16 * y + 16, :] = state.astype(bf16)
            out[z, 64 + 8 * y : 72 + 8 * y, :] = side.astype(bf16)
            state = gain * state + got[z, 16 * y : 16 * y + 16, :].astype(f32)
            side = gain * side + got[z, 64 + 8 * y : 72 + 8 * y, :].astype(f32)


def scan_bwd_kernel(got, gains, out):
    nz, ny = got.shape[0], 4
    state = jnp.zeros((8, 128), f32)
    for y in reversed(range(ny)):
        for z in reversed(range(nz)):
            out[z, 8 * y : 8 * y + 8, :] = state.astype(bf16)
            state = gains[y * nz + z][None] * state + got[z, 8 * y : 8 * y + 8, :].astype(f32)
    up = jnp.sum(got[:, 32:48, :].astype(f32), axis=0).astype(bf16)
    out[:, 32:48, :] = jnp.broadcast_to(up[None], (nz, 16, 128))


def attn_kernel(s_in, lift, logs, kvql_hbm, qpre_hbm, bundle_hbm, send, back_hbm, kvql, qpre, bundle, back, sems):
    ny = kvql.shape[0]
    copies = begin(
        [(kvql_hbm, kvql), (bundle_hbm.at[:, 0:48, :], bundle), (qpre_hbm, qpre)], sems
    )
    cum = running(logs[...])
    square = (cum.shape[1], cum.shape[1])
    causal = lax.broadcasted_iota(jnp.int32, square, 1) <= lax.broadcasted_iota(jnp.int32, square, 0)
    every = range(ny)
    ahead, dec = [], []
    for n in every:
        sums = down_rows(cum[n : n + 1, :])
        ahead.append(jnp.exp(sums))
        spread = jnp.concatenate([sums, sums], axis=1) - cum[n : n + 1, :]
        dec.append(jnp.where(causal, jnp.exp(jnp.where(causal, spread, 0.0)), 0.0))
    s = [s_in[:, n * 16 : n * 16 + 16, :].reshape(128, 128) for n in every]
    side = [
        s_in[:, 64 + n * 8 : 72 + n * 8, :].astype(f32).reshape(64, 128).astype(bf16) for n in every
    ]
    copies[0].wait()
    k, v, q, low = ([kvql[n, i] for n in every] for i in range(4))
    mixed = [(dot_t(q[n], k[n]) * dec[n]).astype(bf16) for n in every]
    attn = [dot(mixed[n], v[n]) + ahead[n] * dot(q[n], s[n]) for n in every]
    copies[1].wait()
    d = []
    for n in every:
        inv = lax.rsqrt(jnp.mean(attn[n] * attn[n], axis=-1, keepdims=True) + eps_norm)
        normed = attn[n] * inv
        parts = []
        for b in (2 * n, 2 * n + 1):
            parts += [bundle[b, :, 0:128], bundle[b, :, 128:256], bundle[b, 0:32, 256:384]]
        up = jnp.concatenate(parts, axis=0).astype(f32)
        dn = (up - normed * jnp.mean(up * normed, axis=-1, keepdims=True)) * inv
        d.append(dn.astype(bf16))
    carried = [t_dot((q[n].astype(f32) * ahead[n]).astype(bf16), d[n]).astype(bf16) for n in every]
    dm = [(dot_t(d[n], v[n]) * dec[n]).astype(bf16) for n in every]
    cross = sum(dot(side[n], carried[n]) for n in every)
    for n in every:
        image = dot_t(lift[1], carried[n])[64:].reshape(-1, 8, 128)
        send[:, n * 8 : n * 8 + 8, :] = image.astype(bf16)
    dv = [t_dot(mixed[n], d[n]).astype(bf16) for n in every]
    dq = [dot(dm[n], k[n]) + ahead[n] * dot_t(d[n], s[n]) for n in every]
    copies[2].wait()
    for n in every:
        u = qpre[n]
        sig = jax.nn.sigmoid(u)
        dq[n] = (dq[n] * (sig * (1.0 + u * (1.0 - sig)))).astype(bf16)
    for n in every:
        back[n] = adapter_scale * (dot_t(dq[n], lift[0]) + dot_t(dv[n], lift[1]))
    store = begin([(back, back_hbm)], sems, 3)[0]
    total_q = sum(t_dot(low[n], dq[n]) for n in every)
    total_v = sum(t_dot(low[n], dv[n]) for n in every)
    up = adapter_scale * jnp.concatenate([total_q[:64], total_v[64:] + cross], axis=0)
    send[:, 32:48, :] = up.astype(bf16).reshape(-1, 16, 128)
    store.wait()


def final_kernel(ids, r_in, logs, kvql_hbm, back_hbm, tok_hbm, keep, give, k, back, tok, acc, terms, sems):
    ny = k.shape[0]
    blocks, own, width = tok.shape
    copies = begin([(kvql_hbm.at[:, 0], k), (back_hbm, back)], sems)
    parts = begin([(tok_hbm.at[b], tok.at[b]) for b in range(blocks)], sems, 2)
    cum = running(logs[...])
    tails = []
    for n in range(ny):
        sums = down_rows(cum[n : n + 1, :])
        tails.append(adapter_scale * jnp.exp(sums[255:256, :] - sums))
    rs = []
    for n in range(ny):
        r = r_in[:, n * 8 : n * 8 + 8, :].astype(f32).reshape(64, 128)
        rs.append(jnp.concatenate([jnp.zeros((64, 128), f32), r], axis=0).astype(bf16))
    up = r_in[:, 32:48, :].reshape(128, 128)
    give[16] = up[:112]
    give[17, :16] = up[112:]
    give[17, 16:] = jnp.zeros((96, 128), bf16)
    for copy in copies:
        copy.wait()
    small = [(back[n] + tails[n] * dot_t(k[n], rs[n])).T.astype(bf16) for n in range(ny)]
    small = [jnp.concatenate(small[i : i + 2], axis=1) for i in (0, 2)]
    half = blocks // 2
    wide = width // 4
    per = keep.shape[1] // 8
    first = ids[1] == 0
    for part in parts[:half]:
        part.wait()
    for y in range(4):
        m = slice(y * wide, y * wide + wide)
        acc[:, m] = dot(small[0], tok[:half, :, m].reshape(half * own, wide))
    for part in parts[half:]:
        part.wait()
    for y in range(4):
        m = slice(y * wide, y * wide + wide)
        terms[m, :] = (acc[:, m] + dot(small[1], tok[half:, :, m].reshape(half * own, wide))).T
        for x in range(4):
            halves = []
            for c in range(2):
                base = ((y * 16 + c) * 4 + x) * per
                rows = [terms[pl.ds(base + r, 8, stride=8 * per), :] for r in range(per)]
                halves.append(jnp.concatenate(rows, axis=0))
            b = y * 4 + x
            keep[b] = jnp.where(first, halves[0], halves[1])
            give[b] = jnp.where(first, halves[1], halves[0]).astype(bf16)


def add_kernel(keep_hbm, give, got, out, pair, keep, sems):
    copies = begin([(keep_hbm.at[4 * i : 4 * i + 4], keep.at[4 * i : 4 * i + 4]) for i in range(4)], sems)
    for i, ref in enumerate((give, got)):
        pair[i, :112] = ref[16]
        pair[i, 112:] = ref[17, :16]
    for i, copy in enumerate(copies):
        copy.wait()
        rows = slice(4 * i, 4 * i + 4)
        out[rows] = (keep[rows] + got[rows].astype(f32)).astype(bf16)


def fold_kernel(got, out, tmp):
    tmp[...] = jnp.sum(got[...].astype(f32), axis=0)
    nz = out.shape[0]
    per = tmp.shape[0] // nz
    for z in range(nz):
        out[z] = jnp.concatenate(
            [tmp[pl.ds(z, per, stride=nz), :], jnp.zeros((out.shape[1] - per, 128), f32)], axis=0
        ).astype(bf16)


def last_kernel(got, out):
    out[...] = jnp.sum(got[...].astype(f32), axis=0)[: out.shape[0]]


def up_kernel(ids, pair, *rest):
    pieces, out = rest[:-1], rest[-1]
    y, c = ids[0], ids[1]

    def put(yy, cc, val):
        out[:, pl.ds(pl.multiple_of((yy * 2 + cc) * 128, 128), 128)] = val.astype(f32)

    put(y, c, pair[0])
    put(y, 1 - c, pair[1])
    for i, rel in enumerate((3, 1, 2)):
        yy = lax.rem(y + rel, 4)
        put(yy, c, pieces[i][0])
        put(yy, 1 - c, pieces[i][1])


def layer(tokens, wq, wk, wv, down, lift, decay, grad):
    own, width = tokens.shape
    rank = lift.shape[1]
    heads = decay.shape[0]
    hk = wq.shape[1] // heads
    group = ("y", "c")
    ny, nz, nc, nx = (lax.axis_size(a) for a in ("y", "z", "c", "x"))
    ids = jnp.stack([lax.axis_index(a) for a in ("y", "c", "z")]).astype(jnp.int32)
    head = lax.axis_index("y") * nc + lax.axis_index("c")
    rows = wq.shape[0]
    span = nc * own
    ring = lambda v, s, a="y", n=ny: lax.ppermute(v, a, [(i, (i + s) % n) for i in range(n)])
    swap = lambda v: lax.ppermute(v, "c", [(0, 1), (1, 0)])
    DMA = pltpu.SemaphoreType.DMA

    below = ring(tokens, 1)
    above = ring(tokens, -1)
    far0 = ring(below[: own // 2], 1)
    far1 = ring(above[own // 2 :], -1)
    pieces = []
    for p in (tokens, below, above, far0, far1):
        pieces += [p, swap(p)]

    bundle = call(
        pack_kernel, shape((heads, 48 + rows, 3 * hk)), wk, wv, wq, grad, decay,
        specs=[HBM] * 5,
        mib=60,
        scratch=[pltpu.VMEM(wk.shape, bf16)] * 3
        + [pltpu.VMEM(grad.shape, bf16), pltpu.VMEM(decay.shape, f32), DMA((5,))],
    )
    bundle = lax.all_to_all(bundle, group, 0, 0, tiled=True)
    w = bundle[:, 48:].reshape(heads * rows, 3 * hk)
    weights, ahead, behind = [w], w, w
    for _ in range(nz // 2 - 1):
        ahead = ring(ahead, 1, "z", nz)
        behind = ring(behind, -1, "z", nz)
        weights += [ahead, behind]
    half = heads * rows // 2
    weights.append(ring(ahead[:half], 1, "z", nz))
    weights.append(ring(behind[half:], -1, "z", nz))
    deep = nc * rows
    weights = [p.reshape(-1, deep, 3 * hk) for p in weights]

    logs = bundle[:, 32:35, 2 * hk :].astype(f32)
    logs = (logs[:, 0] + (logs[:, 1] + logs[:, 2])).reshape(ny, span)
    lift = lax.dynamic_slice_in_dim(lift, head * hk, hk, 2)
    zero = jnp.zeros((rank, hk), bf16)
    lift = jnp.stack([jnp.concatenate([lift[0], zero]), jnp.concatenate([zero, lift[1]])])

    kvql, qpre, tok, send = call(
        project_kernel,
        (
            shape((ny, 4, span, hk)), shape((ny, span, hk), f32),
            shape((heads, own, width)), shape((nz, 112, hk)),
        ),
        ids, down.reshape(ny, nz, deep, 2 * rank), *weights, *pieces, lift, logs,
        mib=60,
        specs=[SMEM] + [HBM] * 20 + [VMEM] * 2,
        out_specs=(HBM, HBM, HBM, VMEM),
        scratch=[
            pltpu.VMEM((ny, nz, deep, 3 * hk + 2 * rank), bf16),
            pltpu.VMEM((heads, own, width), bf16),
            pltpu.VMEM((ny, 4, span, hk), bf16),
            pltpu.VMEM((ny, span, hk), f32),
            pltpu.VMEM((ny, span, hk), f32),
            DMA((32,)),
        ],
    )

    got = lax.all_to_all(send, "z", 0, 0, tiled=True)
    scanned, gains = call(scan_fwd_kernel, (shape((nz, 96, hk)), shape((nz * ny, hk), f32)), got)
    s_in = lax.all_to_all(scanned, "z", 0, 0, tiled=True)

    send, back = call(
        attn_kernel,
        (shape((nz, 48, hk)), shape((ny, span, hk), f32)),
        s_in, lift, logs, kvql, qpre, bundle,
        mib=60,
        specs=[VMEM] * 3 + [HBM] * 3,
        out_specs=(VMEM, HBM),
        scratch=[
            pltpu.VMEM((ny, 4, span, hk), bf16),
            pltpu.VMEM((ny, span, hk), f32),
            pltpu.VMEM((heads, 48, 3 * hk), bf16),
            pltpu.VMEM((ny, span, hk), f32),
            DMA((4,)),
        ],
    )
    got = lax.all_to_all(send, "z", 0, 0, tiled=True)
    scanned = call(scan_bwd_kernel, shape((nz, 48, hk)), got, gains)
    r_in = lax.all_to_all(scanned, "z", 0, 0, tiled=True)

    out_rows = width // (ny * nz * nc * nx)
    keep, give = call(
        final_kernel,
        (
            shape((ny * nx, nz * out_rows, hk), f32),
            shape((ny * nx + 2, nz * out_rows, hk)),
        ),
        ids, r_in, logs, kvql, back, tok,
        specs=[SMEM] + [VMEM] * 2 + [HBM] * 3,
        scratch=[
            pltpu.VMEM((ny, span, hk), bf16),
            pltpu.VMEM((ny, span, hk), f32),
            pltpu.VMEM((heads, own, width), bf16),
            pltpu.VMEM((2 * rank, width), f32),
            pltpu.VMEM((width, 2 * rank), f32),
            DMA((10,)),
        ],
        mib=60,
    )
    down_terms, pair = call(
        add_kernel,
        (shape(keep.shape), shape((2, 2 * rank, hk))),
        keep, give, swap(give),
        specs=[HBM, VMEM, VMEM],
        scratch=[pltpu.VMEM(keep.shape, f32), DMA((4,))],
    )
    ups = [ring(pair, 1), ring(pair, -1), ring(pair, 2)]
    down_terms = lax.all_to_all(down_terms, ("y", "x"), 0, 0, tiled=True)
    down_terms = call(
        fold_kernel, shape((nz, 16, hk)), down_terms,
        scratch=[pltpu.VMEM((nz * out_rows, hk), f32)],
    )
    down_terms = lax.all_to_all(down_terms, "z", 0, 0, tiled=True)
    grad_down = call(last_kernel, shape((out_rows, hk), f32), down_terms)
    grad_up = call(
        up_kernel, shape((2 * rank, heads * hk), f32), ids, pair, *ups,
        specs=[SMEM] + [VMEM] * 4,
    )
    return (grad_down, grad_up.reshape(2, rank, heads * hk))


def solution(mesh):
    n_mp = mesh.shape["mp"]
    wide = Mesh(mesh.devices.reshape(4, 8, 2, n_mp), ("y", "z", "c", "x"))
    seq = ("y", "z", "c")
    return jax.shard_map(
        layer,
        mesh=wide,
        in_specs=(
            P(seq, None),
            P(seq, "x"),
            P(seq, "x"),
            P(seq, "x"),
            P(),
            P(None, None, "x"),
            P("x", seq),
            P(seq, "x"),
        ),
        out_specs=(P(("y", "z", "c", "x"), None), P(None, None, "x")),
        check_vma=False,
    )
```

```python
import jax
import jax.numpy as jnp
from jax import lax
from jax.experimental import pallas as pl
from jax.experimental.pallas import tpu as pltpu
from jax.sharding import Mesh, PartitionSpec as P


bf16, f32 = jnp.bfloat16, jnp.float32
adapter_scale = 2.0
eps_norm = 1e-06
VMEM = pl.BlockSpec(memory_space=pltpu.VMEM)
SMEM = pl.BlockSpec(memory_space=pltpu.SMEM)
ANY = pl.BlockSpec(memory_space=pl.ANY)


def dot(a, b):
    return jnp.dot(a, b, preferred_element_type=f32)


def dot_t(a, b):
    return lax.dot_general(a, b, (((1,), (1,)), ((), ())), preferred_element_type=f32)


def t_dot(a, b):
    return lax.dot_general(a, b, (((0,), (0,)), ((), ())), preferred_element_type=f32)


def shape(dims, dtype=bf16):
    return jax.ShapeDtypeStruct(dims, dtype)


HBM = pl.BlockSpec(memory_space=pltpu.MemorySpace.HBM)


def call(kernel, outs, *args, mib=6, specs=None, out_specs=None, scratch=()):
    return pl.pallas_call(
        kernel,
        out_shape=outs,
        in_specs=specs or [VMEM] * len(args),
        out_specs=out_specs or jax.tree.map(lambda _: VMEM, outs),
        scratch_shapes=scratch,
        compiler_params=pltpu.CompilerParams(vmem_limit_bytes=mib << 20),
    )(*args)


def begin(pairs, sems, first=0):
    copies = [pltpu.make_async_copy(s, d, sems.at[first + i]) for i, (s, d) in enumerate(pairs)]
    for copy in copies:
        copy.start()
    return copies


def split3(d):
    hi = d.astype(bf16).astype(f32)
    mid = (d - hi).astype(bf16).astype(f32)
    return hi, mid, (d - hi - mid).astype(bf16).astype(f32)


def running(logs):
    chunks, n = logs.shape
    parts = jnp.concatenate(list(split3(logs)) + [jnp.zeros((16 - 3 * chunks, n), f32)], axis=0)
    ones = lax.broadcasted_iota(jnp.int32, (n, n), 0) <= lax.broadcasted_iota(jnp.int32, (n, n), 1)
    sums = dot(parts.astype(bf16), ones.astype(f32).astype(bf16))
    return sums[:chunks] + (sums[chunks : 2 * chunks] + sums[2 * chunks : 3 * chunks])


def down_rows(row):
    return jnp.broadcast_to(row, (128, row.shape[1])).T


def pack_kernel(a_hbm, b_hbm, c_hbm, grad_hbm, decay_hbm, out, a, b, c, grad, decay, sems):
    src = (decay_hbm, grad_hbm, a_hbm, b_hbm, c_hbm)
    copies = begin(list(zip(src, (decay, grad, a, b, c))), sems)
    for copy in copies:
        copy.wait()
    hi, mid, lo = split3(decay[...])
    zero = jnp.zeros((13, 128), f32)
    for h in range(out.shape[0]):
        lanes = slice(h * 128, h * 128 + 128)
        out[h, 0:48, 0:128] = grad[0:48, lanes]
        out[h, 0:48, 128:256] = grad[48:96, lanes]
        out[h, 0:32, 256:384] = grad[96:128, lanes]
        logs = jnp.concatenate([hi[h : h + 1], mid[h : h + 1], lo[h : h + 1], zero], axis=0)
        out[h, 32:48, 256:384] = logs.astype(bf16)
        for i, m in enumerate((a, b, c)):
            out[h, 48:, i * 128 : (i + 1) * 128] = m[:, lanes]


def project_kernel(ids, down, *rest):
    weights, pieces, rest = rest[:9], rest[9:19], rest[19:]
    lift, logs, kvql_hbm, qpre_hbm, tok_hbm, send, wbuf, tok, kvql, qpre, tail, sems = rest
    ny, nz, _, wide = wbuf.shape
    y, c, z = ids[0], ids[1], ids[2]
    width = tok.shape[2]
    pairs = [(down, wbuf.at[:, :, :, wide - 128 :])]
    for i, p in enumerate(weights):
        shift = (0, -1, 1, -2, 2, -3, 3, 4, 4)[i]
        src = lax.rem(z + shift + nz, nz)
        span = (slice(0, ny), slice(0, ny // 2), slice(ny // 2, ny))[max(0, i - 6)]
        pairs.append((p, wbuf.at[span, src, :, : wide - 128]))
    half = tok.shape[1] // 2
    for i, p in enumerate(pieces):
        rel = (0, 0, ny - 1, ny - 1, 1, 1, 2, 2, 2, 2)[i]
        core = c if i % 2 == 0 else 1 - c
        dst = tok.at[lax.rem(y + rel, ny) * 2 + core]
        if i >= 6:
            dst = dst.at[half * ((i - 6) // 2) : half * ((i - 6) // 2) + half]
        pairs.append((p, dst))
    copies = begin(pairs, sems)
    ends = []
    cum = running(logs[...])
    for n in range(ny):
        sums = down_rows(cum[n : n + 1, :])
        total = sums[255:256, :]
        tail[n] = jnp.exp(total - sums)
        ends += list(split3(total))
    extra = jnp.concatenate(ends + [jnp.zeros((16 - len(ends), 128), f32)], axis=0).astype(bf16)
    send[:, 96:112, :] = jnp.broadcast_to(extra[None], (send.shape[0], 16, 128))
    for i in range(10):
        copies[i].wait()
    stores = []
    for step, (rel, used) in enumerate(
        ((0, (0, 1)), (ny - 1, (2, 3)), (1, (4, 5)), (2, (6, 7, 8, 9)))
    ):
        for i in used:
            copies[10 + i].wait()
        n = lax.rem(y + rel, ny)
        two = pl.ds(n * 2, 2)
        stores += begin([(tok.at[two], tok_hbm.at[two])], sems, 20 + 3 * step)
        acc = dot(tok[two].reshape(256, width), wbuf[...].reshape(width, wide))
        low = acc[:, 384:].astype(bf16)
        u = acc[:, :128]
        k = (u * jax.nn.sigmoid(u)).astype(bf16)
        v = (acc[:, 128:256] + adapter_scale * dot(low, lift[1])).astype(bf16)
        u = acc[:, 256:384] + adapter_scale * dot(low, lift[0])
        q = (u * jax.nn.sigmoid(u)).astype(bf16)
        faded = (k.astype(f32) * tail[n]).astype(bf16)
        local = t_dot(faded, v).astype(bf16).reshape(-1, 16, 128)
        send[:, pl.ds(pl.multiple_of(n * 16, 16), 16), :] = local
        side = t_dot(low, faded)[64:].reshape(-1, 8, 128)
        send[:, pl.ds(pl.multiple_of(64 + n * 8, 8), 8), :] = side.astype(bf16)
        for i, m in enumerate((k, v, q, low)):
            kvql[step, i] = m
        qpre[step] = u
        stores += begin(
            [(kvql.at[step], kvql_hbm.at[n]), (qpre.at[step], qpre_hbm.at[n])], sems, 21 + 3 * step
        )
    for copy in stores:
        copy.wait()


def scan_fwd_kernel(got, out, gains):
    nz, ny = got.shape[0], 4
    logs = got[:, 96:112, :].astype(f32)
    state = jnp.zeros((16, 128), f32)
    side = jnp.zeros((8, 128), f32)
    for y in range(ny):
        for z in range(nz):
            total = logs[z, 3 * y] + (logs[z, 3 * y + 1] + logs[z, 3 * y + 2])
            gain = jnp.exp(total)[None]
            gains[y * nz + z] = gain[0]
            out[z, 16 * y : 16 * y + 16, :] = state.astype(bf16)
            out[z, 64 + 8 * y : 72 + 8 * y, :] = side.astype(bf16)
            state = gain * state + got[z, 16 * y : 16 * y + 16, :].astype(f32)
            side = gain * side + got[z, 64 + 8 * y : 72 + 8 * y, :].astype(f32)


def scan_bwd_kernel(got, gains, out):
    nz, ny = got.shape[0], 4
    state = jnp.zeros((8, 128), f32)
    for y in reversed(range(ny)):
        for z in reversed(range(nz)):
            out[z, 8 * y : 8 * y + 8, :] = state.astype(bf16)
            state = gains[y * nz + z][None] * state + got[z, 8 * y : 8 * y + 8, :].astype(f32)
    up = jnp.sum(got[:, 32:48, :].astype(f32), axis=0).astype(bf16)
    out[:, 32:48, :] = jnp.broadcast_to(up[None], (nz, 16, 128))


def attn_kernel(s_in, lift, logs, kvql_hbm, qpre_hbm, bundle_hbm, send, back_hbm, kvql, qpre, bundle, back, sems):
    ny = kvql.shape[0]
    copies = begin(
        [(kvql_hbm, kvql), (bundle_hbm.at[:, 0:48, :], bundle), (qpre_hbm, qpre)], sems
    )
    cum = running(logs[...])
    square = (cum.shape[1], cum.shape[1])
    causal = lax.broadcasted_iota(jnp.int32, square, 1) <= lax.broadcasted_iota(jnp.int32, square, 0)
    every = range(ny)
    ahead, dec = [], []
    for n in every:
        sums = down_rows(cum[n : n + 1, :])
        ahead.append(jnp.exp(sums))
        spread = jnp.concatenate([sums, sums], axis=1) - cum[n : n + 1, :]
        dec.append(jnp.where(causal, jnp.exp(jnp.where(causal, spread, 0.0)), 0.0))
    s = [s_in[:, n * 16 : n * 16 + 16, :].reshape(128, 128) for n in every]
    side = [
        s_in[:, 64 + n * 8 : 72 + n * 8, :].astype(f32).reshape(64, 128).astype(bf16) for n in every
    ]
    copies[0].wait()
    k, v, q, low = ([kvql[n, i] for n in every] for i in range(4))
    mixed = [(dot_t(q[n], k[n]) * dec[n]).astype(bf16) for n in every]
    attn = [dot(mixed[n], v[n]) + ahead[n] * dot(q[n], s[n]) for n in every]
    copies[1].wait()
    d = []
    for n in every:
        inv = lax.rsqrt(jnp.mean(attn[n] * attn[n], axis=-1, keepdims=True) + eps_norm)
        normed = attn[n] * inv
        parts = []
        for b in (2 * n, 2 * n + 1):
            parts += [bundle[b, :, 0:128], bundle[b, :, 128:256], bundle[b, 0:32, 256:384]]
        up = jnp.concatenate(parts, axis=0).astype(f32)
        dn = (up - normed * jnp.mean(up * normed, axis=-1, keepdims=True)) * inv
        d.append(dn.astype(bf16))
    carried = [t_dot((q[n].astype(f32) * ahead[n]).astype(bf16), d[n]).astype(bf16) for n in every]
    dm = [(dot_t(d[n], v[n]) * dec[n]).astype(bf16) for n in every]
    cross = sum(dot(side[n], carried[n]) for n in every)
    for n in every:
        image = dot_t(lift[1], carried[n])[64:].reshape(-1, 8, 128)
        send[:, n * 8 : n * 8 + 8, :] = image.astype(bf16)
    dv = [t_dot(mixed[n], d[n]).astype(bf16) for n in every]
    dq = [dot(dm[n], k[n]) + ahead[n] * dot_t(d[n], s[n]) for n in every]
    copies[2].wait()
    for n in every:
        u = qpre[n]
        sig = jax.nn.sigmoid(u)
        dq[n] = (dq[n] * (sig * (1.0 + u * (1.0 - sig)))).astype(bf16)
    for n in every:
        back[n] = adapter_scale * (dot_t(dq[n], lift[0]) + dot_t(dv[n], lift[1]))
    store = begin([(back, back_hbm)], sems, 3)[0]
    total_q = sum(t_dot(low[n], dq[n]) for n in every)
    total_v = sum(t_dot(low[n], dv[n]) for n in every)
    up = adapter_scale * jnp.concatenate([total_q[:64], total_v[64:] + cross], axis=0)
    send[:, 32:48, :] = up.astype(bf16).reshape(-1, 16, 128)
    store.wait()


def final_kernel(ids, r_in, logs, kvql_hbm, back_hbm, tok_hbm, keep, give, k, back, tok, acc, terms, sems):
    ny = k.shape[0]
    blocks, own, width = tok.shape
    copies = begin([(kvql_hbm.at[:, 0], k), (back_hbm, back)], sems)
    parts = begin([(tok_hbm.at[b], tok.at[b]) for b in range(blocks)], sems, 2)
    cum = running(logs[...])
    tails = []
    for n in range(ny):
        sums = down_rows(cum[n : n + 1, :])
        tails.append(adapter_scale * jnp.exp(sums[255:256, :] - sums))
    rs = []
    for n in range(ny):
        r = r_in[:, n * 8 : n * 8 + 8, :].astype(f32).reshape(64, 128)
        rs.append(jnp.concatenate([jnp.zeros((64, 128), f32), r], axis=0).astype(bf16))
    up = r_in[:, 32:48, :].reshape(128, 128)
    give[16] = up[:112]
    give[17, :16] = up[112:]
    give[17, 16:] = jnp.zeros((96, 128), bf16)
    for copy in copies:
        copy.wait()
    small = [(back[n] + tails[n] * dot_t(k[n], rs[n])).T.astype(bf16) for n in range(ny)]
    small = [jnp.concatenate(small[i : i + 2], axis=1) for i in (0, 2)]
    half = blocks // 2
    wide = width // 4
    per = keep.shape[1] // 8
    first = ids[1] == 0
    for part in parts[:half]:
        part.wait()
    for y in range(4):
        m = slice(y * wide, y * wide + wide)
        acc[:, m] = dot(small[0], tok[:half, :, m].reshape(half * own, wide))
    for part in parts[half:]:
        part.wait()
    for y in range(4):
        m = slice(y * wide, y * wide + wide)
        terms[m, :] = (acc[:, m] + dot(small[1], tok[half:, :, m].reshape(half * own, wide))).T
        for x in range(4):
            halves = []
            for c in range(2):
                base = ((y * 16 + c) * 4 + x) * per
                rows = [terms[pl.ds(base + r, 8, stride=8 * per), :] for r in range(per)]
                halves.append(jnp.concatenate(rows, axis=0))
            b = y * 4 + x
            keep[b] = jnp.where(first, halves[0], halves[1])
            give[b] = jnp.where(first, halves[1], halves[0]).astype(bf16)


def add_kernel(keep_hbm, give_hbm, got, out, pair, keep, own, sems):
    quarter = [slice(4 * i, 4 * i + 4) for i in range(4)]
    copies = begin([(give_hbm.at[16:18], own)], sems)
    copies += begin([(keep_hbm.at[rows], keep.at[rows]) for rows in quarter], sems, 1)
    pair[1, :112] = got[16]
    pair[1, 112:] = got[17, :16]
    copies[0].wait()
    pair[0, :112] = own[0]
    pair[0, 112:] = own[1, :16]
    for rows, copy in zip(quarter, copies[1:]):
        copy.wait()
        out[rows] = (keep[rows] + got[rows].astype(f32)).astype(bf16)


def fold_kernel(got, out, tmp):
    tmp[...] = jnp.sum(got[...].astype(f32), axis=0)
    nz = out.shape[0]
    per = tmp.shape[0] // nz
    for z in range(nz):
        out[z] = jnp.concatenate(
            [tmp[pl.ds(z, per, stride=nz), :], jnp.zeros((out.shape[1] - per, 128), f32)], axis=0
        ).astype(bf16)


def last_kernel(got, out):
    out[...] = jnp.sum(got[...].astype(f32), axis=0)[: out.shape[0]]


def up_kernel(ids, pair, *rest):
    pieces, out = rest[:-1], rest[-1]
    y, c = ids[0], ids[1]

    def put(yy, cc, val):
        out[:, pl.ds(pl.multiple_of((yy * 2 + cc) * 128, 128), 128)] = val.astype(f32)

    put(y, c, pair[0])
    put(y, 1 - c, pair[1])
    for i, rel in enumerate((3, 1, 2)):
        yy = lax.rem(y + rel, 4)
        put(yy, c, pieces[i][0])
        put(yy, 1 - c, pieces[i][1])


def layer(tokens, wq, wk, wv, down, lift, decay, grad):
    own, width = tokens.shape
    rank = lift.shape[1]
    heads = decay.shape[0]
    hk = wq.shape[1] // heads
    group = ("y", "c")
    ny, nz, nc, nx = (lax.axis_size(a) for a in ("y", "z", "c", "x"))
    ids = jnp.stack([lax.axis_index(a) for a in ("y", "c", "z")]).astype(jnp.int32)
    head = lax.axis_index("y") * nc + lax.axis_index("c")
    rows = wq.shape[0]
    span = nc * own
    ring = lambda v, s, a="y", n=ny: lax.ppermute(v, a, [(i, (i + s) % n) for i in range(n)])
    swap = lambda v: lax.ppermute(v, "c", [(0, 1), (1, 0)])
    DMA = pltpu.SemaphoreType.DMA

    below = ring(tokens, 1)
    above = ring(tokens, -1)
    far0 = ring(below[: own // 2], 1)
    far1 = ring(above[own // 2 :], -1)
    pieces = []
    for p in (tokens, below, above, far0, far1):
        pieces += [p, swap(p)]

    bundle = call(
        pack_kernel, shape((heads, 48 + rows, 3 * hk)), wk, wv, wq, grad, decay,
        specs=[HBM] * 5,
        mib=60,
        scratch=[pltpu.VMEM(wk.shape, bf16)] * 3
        + [pltpu.VMEM(grad.shape, bf16), pltpu.VMEM(decay.shape, f32), DMA((5,))],
    )
    bundle = lax.all_to_all(bundle, group, 0, 0, tiled=True)
    w = bundle[:, 48:].reshape(heads * rows, 3 * hk)
    weights, ahead, behind = [w], w, w
    for _ in range(nz // 2 - 1):
        ahead = ring(ahead, 1, "z", nz)
        behind = ring(behind, -1, "z", nz)
        weights += [ahead, behind]
    half = heads * rows // 2
    weights.append(ring(ahead[:half], 1, "z", nz))
    weights.append(ring(behind[half:], -1, "z", nz))
    deep = nc * rows
    weights = [p.reshape(-1, deep, 3 * hk) for p in weights]

    logs = bundle[:, 32:35, 2 * hk :].astype(f32)
    logs = (logs[:, 0] + (logs[:, 1] + logs[:, 2])).reshape(ny, span)
    lift = lax.dynamic_slice_in_dim(lift, head * hk, hk, 2)
    zero = jnp.zeros((rank, hk), bf16)
    lift = jnp.stack([jnp.concatenate([lift[0], zero]), jnp.concatenate([zero, lift[1]])])

    kvql, qpre, tok, send = call(
        project_kernel,
        (
            shape((ny, 4, span, hk)), shape((ny, span, hk), f32),
            shape((heads, own, width)), shape((nz, 112, hk)),
        ),
        ids, down.reshape(ny, nz, deep, 2 * rank), *weights, *pieces, lift, logs,
        mib=60,
        specs=[SMEM] + [HBM] * 20 + [VMEM] * 2,
        out_specs=(HBM, HBM, HBM, VMEM),
        scratch=[
            pltpu.VMEM((ny, nz, deep, 3 * hk + 2 * rank), bf16),
            pltpu.VMEM((heads, own, width), bf16),
            pltpu.VMEM((ny, 4, span, hk), bf16),
            pltpu.VMEM((ny, span, hk), f32),
            pltpu.VMEM((ny, span, hk), f32),
            DMA((32,)),
        ],
    )

    got = lax.all_to_all(send, "z", 0, 0, tiled=True)
    scanned, gains = call(scan_fwd_kernel, (shape((nz, 96, hk)), shape((nz * ny, hk), f32)), got)
    s_in = lax.all_to_all(scanned, "z", 0, 0, tiled=True)

    send, back = call(
        attn_kernel,
        (shape((nz, 48, hk)), shape((ny, span, hk), f32)),
        s_in, lift, logs, kvql, qpre, bundle,
        mib=60,
        specs=[VMEM] * 3 + [HBM] * 3,
        out_specs=(VMEM, HBM),
        scratch=[
            pltpu.VMEM((ny, 4, span, hk), bf16),
            pltpu.VMEM((ny, span, hk), f32),
            pltpu.VMEM((heads, 48, 3 * hk), bf16),
            pltpu.VMEM((ny, span, hk), f32),
            DMA((4,)),
        ],
    )
    got = lax.all_to_all(send, "z", 0, 0, tiled=True)
    scanned = call(scan_bwd_kernel, shape((nz, 48, hk)), got, gains)
    r_in = lax.all_to_all(scanned, "z", 0, 0, tiled=True)

    out_rows = width // (ny * nz * nc * nx)
    keep, give = call(
        final_kernel,
        (
            shape((ny * nx, nz * out_rows, hk), f32),
            shape((ny * nx + 2, nz * out_rows, hk)),
        ),
        ids, r_in, logs, kvql, back, tok,
        specs=[SMEM] + [VMEM] * 2 + [HBM] * 3,
        scratch=[
            pltpu.VMEM((ny, span, hk), bf16),
            pltpu.VMEM((ny, span, hk), f32),
            pltpu.VMEM((heads, own, width), bf16),
            pltpu.VMEM((2 * rank, width), f32),
            pltpu.VMEM((width, 2 * rank), f32),
            DMA((10,)),
        ],
        mib=60,
    )
    down_terms, pair = call(
        add_kernel,
        (shape(keep.shape), shape((2, 2 * rank, hk))),
        keep, give, swap(give),
        specs=[HBM, HBM, VMEM],
        mib=60,
        scratch=[
            pltpu.VMEM(keep.shape, f32),
            pltpu.VMEM((2,) + keep.shape[1:], bf16),
            DMA((5,)),
        ],
    )
    ups = [ring(pair, i) for i in (1, 3, 2)]
    down_terms = lax.all_to_all(down_terms, ("y", "x"), 0, 0, tiled=True)
    down_terms = call(
        fold_kernel, shape((nz, 16, hk)), down_terms,
        scratch=[pltpu.VMEM((nz * out_rows, hk), f32)],
    )
    down_terms = lax.all_to_all(down_terms, "z", 0, 0, tiled=True)
    grad_down = call(last_kernel, shape((out_rows, hk), f32), down_terms)
    grad_up = call(
        up_kernel, shape((2 * rank, heads * hk), f32), ids, pair, *ups,
        specs=[SMEM] + [VMEM] * 4,
    )
    return (grad_down, grad_up.reshape(2, rank, heads * hk))


def solution(mesh):
    n_mp = mesh.shape["mp"]
    wide = Mesh(mesh.devices.reshape(4, 8, 2, n_mp), ("y", "z", "c", "x"))
    seq = ("y", "z", "c")
    return jax.shard_map(
        layer,
        mesh=wide,
        in_specs=(
            P(seq, None),
            P(seq, "x"),
            P(seq, "x"),
            P(seq, "x"),
            P(),
            P(None, None, "x"),
            P("x", seq),
            P(seq, "x"),
        ),
        out_specs=(P(("y", "z", "c", "x"), None), P(None, None, "x")),
        check_vma=False,
    )
```

```python
import jax
import jax.numpy as jnp
from jax import lax
from jax.experimental import pallas as pl
from jax.experimental.pallas import tpu as pltpu
from jax.sharding import Mesh, PartitionSpec as P


bf16, f32 = jnp.bfloat16, jnp.float32
adapter_scale = 2.0
eps_norm = 1e-06
VMEM = pl.BlockSpec(memory_space=pltpu.VMEM)
SMEM = pl.BlockSpec(memory_space=pltpu.SMEM)
ANY = pl.BlockSpec(memory_space=pl.ANY)


def dot(a, b):
    return jnp.dot(a, b, preferred_element_type=f32)


def dot_t(a, b):
    return lax.dot_general(a, b, (((1,), (1,)), ((), ())), preferred_element_type=f32)


def t_dot(a, b):
    return lax.dot_general(a, b, (((0,), (0,)), ((), ())), preferred_element_type=f32)


def shape(dims, dtype=bf16):
    return jax.ShapeDtypeStruct(dims, dtype)


HBM = pl.BlockSpec(memory_space=pltpu.MemorySpace.HBM)


def call(kernel, outs, *args, mib=6, specs=None, out_specs=None, scratch=()):
    return pl.pallas_call(
        kernel,
        out_shape=outs,
        in_specs=specs or [VMEM] * len(args),
        out_specs=out_specs or jax.tree.map(lambda _: VMEM, outs),
        scratch_shapes=scratch,
        compiler_params=pltpu.CompilerParams(vmem_limit_bytes=mib << 20),
    )(*args)


def begin(pairs, sems, first=0):
    copies = [pltpu.make_async_copy(s, d, sems.at[first + i]) for i, (s, d) in enumerate(pairs)]
    for copy in copies:
        copy.start()
    return copies


def split3(d):
    hi = d.astype(bf16).astype(f32)
    mid = (d - hi).astype(bf16).astype(f32)
    return hi, mid, (d - hi - mid).astype(bf16).astype(f32)


def running(logs):
    chunks, n = logs.shape
    parts = jnp.concatenate(list(split3(logs)) + [jnp.zeros((16 - 3 * chunks, n), f32)], axis=0)
    ones = lax.broadcasted_iota(jnp.int32, (n, n), 0) <= lax.broadcasted_iota(jnp.int32, (n, n), 1)
    sums = dot(parts.astype(bf16), ones.astype(f32).astype(bf16))
    return sums[:chunks] + (sums[chunks : 2 * chunks] + sums[2 * chunks : 3 * chunks])


def down_rows(row):
    return jnp.broadcast_to(row, (128, row.shape[1])).T


def pack_kernel(a_hbm, b_hbm, c_hbm, grad_hbm, decay_hbm, out, a, b, c, grad, decay, sems):
    src = (decay_hbm, grad_hbm, a_hbm, b_hbm, c_hbm)
    copies = begin(list(zip(src, (decay, grad, a, b, c))), sems)
    for copy in copies:
        copy.wait()
    hi, mid, lo = split3(decay[...])
    zero = jnp.zeros((13, 128), f32)
    for h in range(out.shape[0]):
        lanes = slice(h * 128, h * 128 + 128)
        out[h, 0:48, 0:128] = grad[0:48, lanes]
        out[h, 0:48, 128:256] = grad[48:96, lanes]
        out[h, 0:32, 256:384] = grad[96:128, lanes]
        logs = jnp.concatenate([hi[h : h + 1], mid[h : h + 1], lo[h : h + 1], zero], axis=0)
        out[h, 32:48, 256:384] = logs.astype(bf16)
        for i, m in enumerate((a, b, c)):
            out[h, 48:, i * 128 : (i + 1) * 128] = m[:, lanes]


def project_kernel(ids, down, *rest):
    weights, pieces, rest = rest[:9], rest[9:19], rest[19:]
    lift, logs, kvql_hbm, qpre_hbm, tok_hbm, send, wbuf, tok, kvql, qpre, tail, sems = rest
    ny, nz, _, wide = wbuf.shape
    y, c, z = ids[0], ids[1], ids[2]
    width = tok.shape[2]
    pairs = [(down, wbuf.at[:, :, :, wide - 128 :])]
    for i, p in enumerate(weights):
        shift = (0, -1, 1, -2, 2, -3, 3, 4, 4)[i]
        src = lax.rem(z + shift + nz, nz)
        span = (slice(0, ny), slice(0, ny // 2), slice(ny // 2, ny))[max(0, i - 6)]
        pairs.append((p, wbuf.at[span, src, :, : wide - 128]))
    half = tok.shape[1] // 2
    for i, p in enumerate(pieces):
        rel = (0, 0, ny - 1, ny - 1, 1, 1, 2, 2, 2, 2)[i]
        core = c if i % 2 == 0 else 1 - c
        dst = tok.at[lax.rem(y + rel, ny) * 2 + core]
        if i >= 6:
            dst = dst.at[half * ((i - 6) // 2) : half * ((i - 6) // 2) + half]
        pairs.append((p, dst))
    copies = begin(pairs, sems)
    ends = []
    cum = running(logs[...])
    for n in range(ny):
        sums = down_rows(cum[n : n + 1, :])
        total = sums[255:256, :]
        tail[n] = jnp.exp(total - sums)
        ends += list(split3(total))
    extra = jnp.concatenate(ends + [jnp.zeros((16 - len(ends), 128), f32)], axis=0).astype(bf16)
    send[:, 96:112, :] = jnp.broadcast_to(extra[None], (send.shape[0], 16, 128))
    for i in range(10):
        copies[i].wait()
    stores = []
    for step, (rel, used) in enumerate(
        ((0, (0, 1)), (ny - 1, (2, 3)), (1, (4, 5)), (2, (6, 7, 8, 9)))
    ):
        for i in used:
            copies[10 + i].wait()
        n = lax.rem(y + rel, ny)
        two = pl.ds(n * 2, 2)
        stores += begin([(tok.at[two], tok_hbm.at[two])], sems, 20 + 3 * step)
        acc = dot(tok[two].reshape(256, width), wbuf[...].reshape(width, wide))
        low = acc[:, 384:].astype(bf16)
        u = acc[:, :128]
        k = (u * jax.nn.sigmoid(u)).astype(bf16)
        v = (acc[:, 128:256] + adapter_scale * dot(low, lift[1])).astype(bf16)
        u = acc[:, 256:384] + adapter_scale * dot(low, lift[0])
        q = (u * jax.nn.sigmoid(u)).astype(bf16)
        faded = (k.astype(f32) * tail[n]).astype(bf16)
        local = t_dot(faded, v).astype(bf16).reshape(-1, 16, 128)
        send[:, pl.ds(pl.multiple_of(n * 16, 16), 16), :] = local
        side = t_dot(low, faded)[64:].reshape(-1, 8, 128)
        send[:, pl.ds(pl.multiple_of(64 + n * 8, 8), 8), :] = side.astype(bf16)
        for i, m in enumerate((k, v, q, low)):
            kvql[step, i] = m
        qpre[step] = u
        stores += begin(
            [(kvql.at[step], kvql_hbm.at[n]), (qpre.at[step], qpre_hbm.at[n])], sems, 21 + 3 * step
        )
    for copy in stores:
        copy.wait()


def scan_fwd_kernel(got, out, gains):
    nz, ny = got.shape[0], 4
    logs = got[:, 96:112, :].astype(f32)
    state = jnp.zeros((16, 128), f32)
    side = jnp.zeros((8, 128), f32)
    for y in range(ny):
        for z in range(nz):
            total = logs[z, 3 * y] + (logs[z, 3 * y + 1] + logs[z, 3 * y + 2])
            gain = jnp.exp(total)[None]
            gains[y * nz + z] = gain[0]
            out[z, 16 * y : 16 * y + 16, :] = state.astype(bf16)
            out[z, 64 + 8 * y : 72 + 8 * y, :] = side.astype(bf16)
            state = gain * state + got[z, 16 * y : 16 * y + 16, :].astype(f32)
            side = gain * side + got[z, 64 + 8 * y : 72 + 8 * y, :].astype(f32)


def scan_bwd_kernel(got, gains, out):
    nz, ny = got.shape[0], 4
    state = jnp.zeros((8, 128), f32)
    for y in reversed(range(ny)):
        for z in reversed(range(nz)):
            out[z, 8 * y : 8 * y + 8, :] = state.astype(bf16)
            state = gains[y * nz + z][None] * state + got[z, 8 * y : 8 * y + 8, :].astype(f32)
    up = jnp.sum(got[:, 32:48, :].astype(f32), axis=0).astype(bf16)
    out[:, 32:48, :] = jnp.broadcast_to(up[None], (nz, 16, 128))


def attn_kernel(s_in, lift, logs, kvql_hbm, qpre_hbm, bundle_hbm, send, back_hbm, kvql, qpre, bundle, back, sems):
    ny = kvql.shape[0]
    copies = begin(
        [(kvql_hbm, kvql), (bundle_hbm.at[:, 0:48, :], bundle), (qpre_hbm, qpre)], sems
    )
    cum = running(logs[...])
    square = (cum.shape[1], cum.shape[1])
    causal = lax.broadcasted_iota(jnp.int32, square, 1) <= lax.broadcasted_iota(jnp.int32, square, 0)
    every = range(ny)
    ahead, dec = [], []
    for n in every:
        sums = down_rows(cum[n : n + 1, :])
        ahead.append(jnp.exp(sums))
        spread = jnp.concatenate([sums, sums], axis=1) - cum[n : n + 1, :]
        dec.append(jnp.where(causal, jnp.exp(jnp.where(causal, spread, 0.0)), 0.0))
    s = [s_in[:, n * 16 : n * 16 + 16, :].reshape(128, 128) for n in every]
    side = [
        s_in[:, 64 + n * 8 : 72 + n * 8, :].astype(f32).reshape(64, 128).astype(bf16) for n in every
    ]
    copies[0].wait()
    k, v, q, low = ([kvql[n, i] for n in every] for i in range(4))
    mixed = [(dot_t(q[n], k[n]) * dec[n]).astype(bf16) for n in every]
    attn = [dot(mixed[n], v[n]) + ahead[n] * dot(q[n], s[n]) for n in every]
    copies[1].wait()
    d = []
    for n in every:
        inv = lax.rsqrt(jnp.mean(attn[n] * attn[n], axis=-1, keepdims=True) + eps_norm)
        normed = attn[n] * inv
        parts = []
        for b in (2 * n, 2 * n + 1):
            parts += [bundle[b, :, 0:128], bundle[b, :, 128:256], bundle[b, 0:32, 256:384]]
        up = jnp.concatenate(parts, axis=0).astype(f32)
        dn = (up - normed * jnp.mean(up * normed, axis=-1, keepdims=True)) * inv
        d.append(dn.astype(bf16))
    carried = [t_dot((q[n].astype(f32) * ahead[n]).astype(bf16), d[n]).astype(bf16) for n in every]
    dm = [(dot_t(d[n], v[n]) * dec[n]).astype(bf16) for n in every]
    cross = sum(dot(side[n], carried[n]) for n in every)
    for n in every:
        image = dot_t(lift[1], carried[n])[64:].reshape(-1, 8, 128)
        send[:, n * 8 : n * 8 + 8, :] = image.astype(bf16)
    dv = [t_dot(mixed[n], d[n]).astype(bf16) for n in every]
    dq = [dot(dm[n], k[n]) + ahead[n] * dot_t(d[n], s[n]) for n in every]
    copies[2].wait()
    for n in every:
        u = qpre[n]
        sig = jax.nn.sigmoid(u)
        dq[n] = (dq[n] * (sig * (1.0 + u * (1.0 - sig)))).astype(bf16)
    for n in every:
        back[n] = adapter_scale * (dot_t(dq[n], lift[0]) + dot_t(dv[n], lift[1]))
    store = begin([(back, back_hbm)], sems, 3)[0]
    total_q = sum(t_dot(low[n], dq[n]) for n in every)
    total_v = sum(t_dot(low[n], dv[n]) for n in every)
    up = adapter_scale * jnp.concatenate([total_q[:64], total_v[64:] + cross], axis=0)
    send[:, 32:48, :] = up.astype(bf16).reshape(-1, 16, 128)
    store.wait()


def final_kernel(r_in, logs, kvql_hbm, back_hbm, tok_hbm, out, up, k, back, tok, acc, terms, sems):
    ny = k.shape[0]
    blocks, own, width = tok.shape
    copies = begin([(kvql_hbm.at[:, 0], k), (back_hbm, back)], sems)
    parts = begin([(tok_hbm.at[b], tok.at[b]) for b in range(blocks)], sems, 2)
    cum = running(logs[...])
    tails = []
    for n in range(ny):
        sums = down_rows(cum[n : n + 1, :])
        tails.append(adapter_scale * jnp.exp(sums[255:256, :] - sums))
    rs = []
    for n in range(ny):
        r = r_in[:, n * 8 : n * 8 + 8, :].astype(f32).reshape(64, 128)
        rs.append(jnp.concatenate([jnp.zeros((64, 128), f32), r], axis=0).astype(bf16))
    up[...] = r_in[:, 32:48, :].reshape(128, 128)
    for copy in copies:
        copy.wait()
    small = [(back[n] + tails[n] * dot_t(k[n], rs[n])).T.astype(bf16) for n in range(ny)]
    small = [jnp.concatenate(small[i : i + 2], axis=1) for i in (0, 2)]
    half = blocks // 2
    wide = width // 4
    per = out.shape[1] // 8
    for part in parts[:half]:
        part.wait()
    for y in range(4):
        m = slice(y * wide, y * wide + wide)
        acc[:, m] = dot(small[0], tok[:half, :, m].reshape(half * own, wide))
    for part in parts[half:]:
        part.wait()
    for y in range(4):
        m = slice(y * wide, y * wide + wide)
        terms[m, :] = (acc[:, m] + dot(small[1], tok[half:, :, m].reshape(half * own, wide))).T
        for cx in range(8):
            base = (y * 64 + cx) * per
            rows = [terms[pl.ds(base + r, 8, stride=8 * per), :] for r in range(per)]
            out[y * 8 + cx] = jnp.concatenate(rows, axis=0).astype(bf16)


def fold_kernel(got, out, tmp):
    tmp[...] = jnp.sum(got[...].astype(f32), axis=0)
    nz = out.shape[0]
    per = tmp.shape[0] // nz
    for z in range(nz):
        out[z] = jnp.concatenate(
            [tmp[pl.ds(z, per, stride=nz), :], jnp.zeros((out.shape[1] - per, 128), f32)], axis=0
        ).astype(bf16)


def last_kernel(got, out):
    out[...] = jnp.sum(got[...].astype(f32), axis=0)[: out.shape[0]]


def up_kernel(ids, pair, *rest):
    pieces, out = rest[:-1], rest[-1]
    y, c = ids[0], ids[1]

    def put(yy, cc, val):
        out[:, pl.ds(pl.multiple_of((yy * 2 + cc) * 128, 128), 128)] = val.astype(f32)

    put(y, c, pair[0])
    put(y, 1 - c, pair[1])
    for i, rel in enumerate((3, 1, 2)):
        yy = lax.rem(y + rel, 4)
        put(yy, c, pieces[i][0])
        put(yy, 1 - c, pieces[i][1])


def layer(tokens, wq, wk, wv, down, lift, decay, grad):
    own, width = tokens.shape
    rank = lift.shape[1]
    heads = decay.shape[0]
    hk = wq.shape[1] // heads
    group = ("y", "c")
    ny, nz, nc, nx = (lax.axis_size(a) for a in ("y", "z", "c", "x"))
    ids = jnp.stack([lax.axis_index(a) for a in ("y", "c", "z")]).astype(jnp.int32)
    head = lax.axis_index("y") * nc + lax.axis_index("c")
    rows = wq.shape[0]
    span = nc * own
    ring = lambda v, s, a="y", n=ny: lax.ppermute(v, a, [(i, (i + s) % n) for i in range(n)])
    swap = lambda v: lax.ppermute(v, "c", [(0, 1), (1, 0)])
    DMA = pltpu.SemaphoreType.DMA

    below = ring(tokens, 1)
    above = ring(tokens, -1)
    far0 = ring(below[: own // 2], 1)
    far1 = ring(above[own // 2 :], -1)
    pieces = []
    for p in (tokens, below, above, far0, far1):
        pieces += [p, swap(p)]

    bundle = call(
        pack_kernel, shape((heads, 48 + rows, 3 * hk)), wk, wv, wq, grad, decay,
        specs=[HBM] * 5,
        mib=60,
        scratch=[pltpu.VMEM(wk.shape, bf16)] * 3
        + [pltpu.VMEM(grad.shape, bf16), pltpu.VMEM(decay.shape, f32), DMA((5,))],
    )
    bundle = lax.all_to_all(bundle, group, 0, 0, tiled=True)
    w = bundle[:, 48:].reshape(heads * rows, 3 * hk)
    weights, ahead, behind = [w], w, w
    for _ in range(nz // 2 - 1):
        ahead = ring(ahead, 1, "z", nz)
        behind = ring(behind, -1, "z", nz)
        weights += [ahead, behind]
    half = heads * rows // 2
    weights.append(ring(weights[3][:half], 2, "z", nz))
    weights.append(ring(weights[4][half:], -2, "z", nz))
    deep = nc * rows
    weights = [p.reshape(-1, deep, 3 * hk) for p in weights]

    logs = bundle[:, 32:35, 2 * hk :].astype(f32)
    logs = (logs[:, 0] + (logs[:, 1] + logs[:, 2])).reshape(ny, span)
    lift = lax.dynamic_slice_in_dim(lift, head * hk, hk, 2)
    zero = jnp.zeros((rank, hk), bf16)
    lift = jnp.stack([jnp.concatenate([lift[0], zero]), jnp.concatenate([zero, lift[1]])])

    kvql, qpre, tok, send = call(
        project_kernel,
        (
            shape((ny, 4, span, hk)), shape((ny, span, hk), f32),
            shape((heads, own, width)), shape((nz, 112, hk)),
        ),
        ids, down.reshape(ny, nz, deep, 2 * rank), *weights, *pieces, lift, logs,
        mib=60,
        specs=[SMEM] + [HBM] * 20 + [VMEM] * 2,
        out_specs=(HBM, HBM, HBM, VMEM),
        scratch=[
            pltpu.VMEM((ny, nz, deep, 3 * hk + 2 * rank), bf16),
            pltpu.VMEM((heads, own, width), bf16),
            pltpu.VMEM((ny, 4, span, hk), bf16),
            pltpu.VMEM((ny, span, hk), f32),
            pltpu.VMEM((ny, span, hk), f32),
            DMA((32,)),
        ],
    )

    got = lax.all_to_all(send, "z", 0, 0, tiled=True)
    scanned, gains = call(scan_fwd_kernel, (shape((nz, 96, hk)), shape((nz * ny, hk), f32)), got)
    s_in = lax.all_to_all(scanned, "z", 0, 0, tiled=True)

    send, back = call(
        attn_kernel,
        (shape((nz, 48, hk)), shape((ny, span, hk), f32)),
        s_in, lift, logs, kvql, qpre, bundle,
        mib=60,
        specs=[VMEM] * 3 + [HBM] * 3,
        out_specs=(VMEM, HBM),
        scratch=[
            pltpu.VMEM((ny, 4, span, hk), bf16),
            pltpu.VMEM((ny, span, hk), f32),
            pltpu.VMEM((heads, 48, 3 * hk), bf16),
            pltpu.VMEM((ny, span, hk), f32),
            DMA((4,)),
        ],
    )
    got = lax.all_to_all(send, "z", 0, 0, tiled=True)
    scanned = call(scan_bwd_kernel, shape((nz, 48, hk)), got, gains)
    r_in = lax.all_to_all(scanned, "z", 0, 0, tiled=True)

    out_rows = width // (ny * nz * nc * nx)
    down_terms, up = call(
        final_kernel,
        (shape((ny * nc * nx, nz * out_rows, hk)), shape((2 * rank, hk))),
        r_in, logs, kvql, back, tok,
        specs=[VMEM] * 2 + [HBM] * 3,
        scratch=[
            pltpu.VMEM((ny, span, hk), bf16),
            pltpu.VMEM((ny, span, hk), f32),
            pltpu.VMEM((heads, own, width), bf16),
            pltpu.VMEM((2 * rank, width), f32),
            pltpu.VMEM((width, 2 * rank), f32),
            DMA((10,)),
        ],
        mib=60,
    )
    down_terms = lax.all_to_all(down_terms, ("y", "c", "x"), 0, 0, tiled=True)
    pair = jnp.stack([up, swap(up)])
    ups = [ring(pair, 1), ring(pair, -1), ring(pair, 2)]
    down_terms = call(
        fold_kernel, shape((nz, 16, hk)), down_terms,
        scratch=[pltpu.VMEM((nz * out_rows, hk), f32)],
    )
    down_terms = lax.all_to_all(down_terms, "z", 0, 0, tiled=True)
    grad_down = call(last_kernel, shape((out_rows, hk), f32), down_terms)
    grad_up = call(
        up_kernel, shape((2 * rank, heads * hk), f32), ids, pair, *ups,
        specs=[SMEM] + [VMEM] * 4,
    )
    return (grad_down, grad_up.reshape(2, rank, heads * hk))


def solution(mesh):
    n_mp = mesh.shape["mp"]
    wide = Mesh(mesh.devices.reshape(4, 8, 2, n_mp), ("y", "z", "c", "x"))
    seq = ("y", "z", "c")
    return jax.shard_map(
        layer,
        mesh=wide,
        in_specs=(
            P(seq, None),
            P(seq, "x"),
            P(seq, "x"),
            P(seq, "x"),
            P(),
            P(None, None, "x"),
            P("x", seq),
            P(seq, "x"),
        ),
        out_specs=(P(("y", "z", "c", "x"), None), P(None, None, "x")),
        check_vma=False,
    )
```

```python
import jax
import jax.numpy as jnp
from jax import lax
from jax.experimental import pallas as pl
from jax.experimental.pallas import tpu as pltpu
from jax.sharding import Mesh, PartitionSpec as P


bf16, f32 = jnp.bfloat16, jnp.float32
adapter_scale = 2.0
eps_norm = 1e-06
VMEM = pl.BlockSpec(memory_space=pltpu.VMEM)
SMEM = pl.BlockSpec(memory_space=pltpu.SMEM)
ANY = pl.BlockSpec(memory_space=pl.ANY)


def dot(a, b):
    return jnp.dot(a, b, preferred_element_type=f32)


def dot_t(a, b):
    return lax.dot_general(a, b, (((1,), (1,)), ((), ())), preferred_element_type=f32)


def t_dot(a, b):
    return lax.dot_general(a, b, (((0,), (0,)), ((), ())), preferred_element_type=f32)


def shape(dims, dtype=bf16):
    return jax.ShapeDtypeStruct(dims, dtype)


HBM = pl.BlockSpec(memory_space=pltpu.MemorySpace.HBM)


def call(kernel, outs, *args, mib=6, specs=None, out_specs=None, scratch=()):
    return pl.pallas_call(
        kernel,
        out_shape=outs,
        in_specs=specs or [VMEM] * len(args),
        out_specs=out_specs or jax.tree.map(lambda _: VMEM, outs),
        scratch_shapes=scratch,
        compiler_params=pltpu.CompilerParams(vmem_limit_bytes=mib << 20),
    )(*args)


def begin(pairs, sems, first=0):
    copies = [pltpu.make_async_copy(s, d, sems.at[first + i]) for i, (s, d) in enumerate(pairs)]
    for copy in copies:
        copy.start()
    return copies


def split3(d):
    hi = d.astype(bf16).astype(f32)
    mid = (d - hi).astype(bf16).astype(f32)
    return hi, mid, (d - hi - mid).astype(bf16).astype(f32)


def running(logs):
    chunks, n = logs.shape
    parts = jnp.concatenate(list(split3(logs)) + [jnp.zeros((16 - 3 * chunks, n), f32)], axis=0)
    ones = lax.broadcasted_iota(jnp.int32, (n, n), 0) <= lax.broadcasted_iota(jnp.int32, (n, n), 1)
    sums = dot(parts.astype(bf16), ones.astype(f32).astype(bf16))
    return sums[:chunks] + (sums[chunks : 2 * chunks] + sums[2 * chunks : 3 * chunks])


def down_rows(row):
    return jnp.broadcast_to(row, (128, row.shape[1])).T


def pack_kernel(a_hbm, b_hbm, c_hbm, grad_hbm, decay_hbm, out, a, b, c, grad, decay, sems):
    src = (decay_hbm, grad_hbm, a_hbm, b_hbm, c_hbm)
    copies = begin(list(zip(src, (decay, grad, a, b, c))), sems)
    for copy in copies:
        copy.wait()
    hi, mid, lo = split3(decay[...])
    zero = jnp.zeros((13, 128), f32)
    for h in range(out.shape[0]):
        lanes = slice(h * 128, h * 128 + 128)
        out[h, 0:48, 0:128] = grad[0:48, lanes]
        out[h, 0:48, 128:256] = grad[48:96, lanes]
        out[h, 0:32, 256:384] = grad[96:128, lanes]
        logs = jnp.concatenate([hi[h : h + 1], mid[h : h + 1], lo[h : h + 1], zero], axis=0)
        out[h, 32:48, 256:384] = logs.astype(bf16)
        for i, m in enumerate((a, b, c)):
            out[h, 48:, i * 128 : (i + 1) * 128] = m[:, lanes]


def project_kernel(ids, down, *rest):
    weights, pieces, rest = rest[:9], rest[9:19], rest[19:]
    lift, logs, kvql_hbm, qpre_hbm, tok_hbm, send, wbuf, tok, kvql, qpre, tail, sems = rest
    ny, nz, _, wide = wbuf.shape
    y, c, z = ids[0], ids[1], ids[2]
    width = tok.shape[2]
    pairs = [(down, wbuf.at[:, :, :, wide - 128 :])]
    for i, p in enumerate(weights):
        shift = (0, -1, 1, -2, 2, -3, 3, 4, 4)[i]
        src = lax.rem(z + shift + nz, nz)
        span = (slice(0, ny), slice(0, ny // 2), slice(ny // 2, ny))[max(0, i - 6)]
        pairs.append((p, wbuf.at[span, src, :, : wide - 128]))
    half = tok.shape[1] // 2
    for i, p in enumerate(pieces):
        rel = (0, 0, ny - 1, ny - 1, 1, 1, 2, 2, 2, 2)[i]
        core = c if i % 2 == 0 else 1 - c
        dst = tok.at[lax.rem(y + rel, ny) * 2 + core]
        if i >= 6:
            dst = dst.at[half * ((i - 6) // 2) : half * ((i - 6) // 2) + half]
        pairs.append((p, dst))
    copies = begin(pairs, sems)
    ends = []
    cum = running(logs[...])
    for n in range(ny):
        sums = down_rows(cum[n : n + 1, :])
        total = sums[255:256, :]
        tail[n] = jnp.exp(total - sums)
        ends += list(split3(total))
    extra = jnp.concatenate(ends + [jnp.zeros((16 - len(ends), 128), f32)], axis=0).astype(bf16)
    send[:, 96:112, :] = jnp.broadcast_to(extra[None], (send.shape[0], 16, 128))
    for i in range(10):
        copies[i].wait()
    stores = []
    for step, (rel, used) in enumerate(
        ((0, (0, 1)), (ny - 1, (2, 3)), (1, (4, 5)), (2, (6, 7, 8, 9)))
    ):
        for i in used:
            copies[10 + i].wait()
        n = lax.rem(y + rel, ny)
        two = pl.ds(n * 2, 2)
        stores += begin([(tok.at[two], tok_hbm.at[two])], sems, 20 + 3 * step)
        acc = dot(tok[two].reshape(256, width), wbuf[...].reshape(width, wide))
        low = acc[:, 384:].astype(bf16)
        u = acc[:, :128]
        k = (u * jax.nn.sigmoid(u)).astype(bf16)
        v = (acc[:, 128:256] + adapter_scale * dot(low, lift[1])).astype(bf16)
        u = acc[:, 256:384] + adapter_scale * dot(low, lift[0])
        q = (u * jax.nn.sigmoid(u)).astype(bf16)
        faded = (k.astype(f32) * tail[n]).astype(bf16)
        local = t_dot(faded, v).astype(bf16).reshape(-1, 16, 128)
        send[:, pl.ds(pl.multiple_of(n * 16, 16), 16), :] = local
        side = t_dot(low, faded)[64:].reshape(-1, 8, 128)
        send[:, pl.ds(pl.multiple_of(64 + n * 8, 8), 8), :] = side.astype(bf16)
        for i, m in enumerate((k, v, q, low)):
            kvql[step, i] = m
        qpre[step] = u
        stores += begin(
            [(kvql.at[step], kvql_hbm.at[n]), (qpre.at[step], qpre_hbm.at[n])], sems, 21 + 3 * step
        )
    for copy in stores:
        copy.wait()


def scan_fwd_kernel(got, out, gains):
    nz, ny = got.shape[0], 4
    logs = got[:, 96:112, :].astype(f32)
    state = jnp.zeros((16, 128), f32)
    side = jnp.zeros((8, 128), f32)
    for y in range(ny):
        for z in range(nz):
            total = logs[z, 3 * y] + (logs[z, 3 * y + 1] + logs[z, 3 * y + 2])
            gain = jnp.exp(total)[None]
            gains[y * nz + z] = gain[0]
            out[z, 16 * y : 16 * y + 16, :] = state.astype(bf16)
            out[z, 64 + 8 * y : 72 + 8 * y, :] = side.astype(bf16)
            state = gain * state + got[z, 16 * y : 16 * y + 16, :].astype(f32)
            side = gain * side + got[z, 64 + 8 * y : 72 + 8 * y, :].astype(f32)


def scan_bwd_kernel(got, gains, out):
    nz, ny = got.shape[0], 4
    state = jnp.zeros((8, 128), f32)
    for y in reversed(range(ny)):
        for z in reversed(range(nz)):
            out[z, 8 * y : 8 * y + 8, :] = state.astype(bf16)
            state = gains[y * nz + z][None] * state + got[z, 8 * y : 8 * y + 8, :].astype(f32)
    up = jnp.sum(got[:, 32:48, :].astype(f32), axis=0).astype(bf16)
    out[:, 32:48, :] = jnp.broadcast_to(up[None], (nz, 16, 128))


def attn_kernel(s_in, lift, logs, kvql_hbm, qpre_hbm, bundle_hbm, send, back_hbm, kvql, qpre, bundle, back, sems):
    ny = kvql.shape[0]
    copies = begin(
        [(kvql_hbm, kvql), (bundle_hbm.at[:, 0:48, :], bundle), (qpre_hbm, qpre)], sems
    )
    cum = running(logs[...])
    square = (cum.shape[1], cum.shape[1])
    causal = lax.broadcasted_iota(jnp.int32, square, 1) <= lax.broadcasted_iota(jnp.int32, square, 0)
    every = range(ny)
    ahead, dec = [], []
    for n in every:
        sums = down_rows(cum[n : n + 1, :])
        ahead.append(jnp.exp(sums))
        spread = jnp.concatenate([sums, sums], axis=1) - cum[n : n + 1, :]
        dec.append(jnp.where(causal, jnp.exp(jnp.where(causal, spread, 0.0)), 0.0))
    s = [s_in[:, n * 16 : n * 16 + 16, :].reshape(128, 128) for n in every]
    side = [
        s_in[:, 64 + n * 8 : 72 + n * 8, :].astype(f32).reshape(64, 128).astype(bf16) for n in every
    ]
    copies[0].wait()
    k, v, q, low = ([kvql[n, i] for n in every] for i in range(4))
    mixed = [(dot_t(q[n], k[n]) * dec[n]).astype(bf16) for n in every]
    attn = [dot(mixed[n], v[n]) + ahead[n] * dot(q[n], s[n]) for n in every]
    copies[1].wait()
    d = []
    for n in every:
        inv = lax.rsqrt(jnp.mean(attn[n] * attn[n], axis=-1, keepdims=True) + eps_norm)
        normed = attn[n] * inv
        parts = []
        for b in (2 * n, 2 * n + 1):
            parts += [bundle[b, :, 0:128], bundle[b, :, 128:256], bundle[b, 0:32, 256:384]]
        up = jnp.concatenate(parts, axis=0).astype(f32)
        dn = (up - normed * jnp.mean(up * normed, axis=-1, keepdims=True)) * inv
        d.append(dn.astype(bf16))
    carried = [t_dot((q[n].astype(f32) * ahead[n]).astype(bf16), d[n]).astype(bf16) for n in every]
    dm = [(dot_t(d[n], v[n]) * dec[n]).astype(bf16) for n in every]
    cross = sum(dot(side[n], carried[n]) for n in every)
    for n in every:
        image = dot_t(lift[1], carried[n])[64:].reshape(-1, 8, 128)
        send[:, n * 8 : n * 8 + 8, :] = image.astype(bf16)
    dv = [t_dot(mixed[n], d[n]).astype(bf16) for n in every]
    dq = [dot(dm[n], k[n]) + ahead[n] * dot_t(d[n], s[n]) for n in every]
    copies[2].wait()
    for n in every:
        u = qpre[n]
        sig = jax.nn.sigmoid(u)
        dq[n] = (dq[n] * (sig * (1.0 + u * (1.0 - sig)))).astype(bf16)
    for n in every:
        back[n] = adapter_scale * (dot_t(dq[n], lift[0]) + dot_t(dv[n], lift[1]))
    store = begin([(back, back_hbm)], sems, 3)[0]
    total_q = sum(t_dot(low[n], dq[n]) for n in every)
    total_v = sum(t_dot(low[n], dv[n]) for n in every)
    up = adapter_scale * jnp.concatenate([total_q[:64], total_v[64:] + cross], axis=0)
    send[:, 32:48, :] = up.astype(bf16).reshape(-1, 16, 128)
    store.wait()


def final_kernel(r_in, logs, kvql_hbm, back_hbm, tok_hbm, out, up, k, back, tok, acc, terms, sems):
    ny = k.shape[0]
    blocks, own, width = tok.shape
    copies = begin([(kvql_hbm.at[:, 0], k), (back_hbm, back)], sems)
    parts = begin([(tok_hbm.at[b], tok.at[b]) for b in range(blocks)], sems, 2)
    cum = running(logs[...])
    tails = []
    for n in range(ny):
        sums = down_rows(cum[n : n + 1, :])
        tails.append(adapter_scale * jnp.exp(sums[255:256, :] - sums))
    rs = []
    for n in range(ny):
        r = r_in[:, n * 8 : n * 8 + 8, :].astype(f32).reshape(64, 128)
        rs.append(jnp.concatenate([jnp.zeros((64, 128), f32), r], axis=0).astype(bf16))
    up[...] = r_in[:, 32:48, :].reshape(128, 128)
    for copy in copies:
        copy.wait()
    small = [(back[n] + tails[n] * dot_t(k[n], rs[n])).T.astype(bf16) for n in range(ny)]
    small = [jnp.concatenate(small[i : i + 2], axis=1) for i in (0, 2)]
    half = blocks // 2
    wide = width // 4
    per = out.shape[1] // 8
    for part in parts[:half]:
        part.wait()
    for y in range(4):
        m = slice(y * wide, y * wide + wide)
        acc[:, m] = dot(small[0], tok[:half, :, m].reshape(half * own, wide))
    for part in parts[half:]:
        part.wait()
    for y in range(4):
        m = slice(y * wide, y * wide + wide)
        terms[m, :] = (acc[:, m] + dot(small[1], tok[half:, :, m].reshape(half * own, wide))).T
        for cx in range(8):
            base = (y * 64 + cx) * per
            rows = [terms[pl.ds(base + r, 8, stride=8 * per), :] for r in range(per)]
            out[y * 8 + cx] = jnp.concatenate(rows, axis=0).astype(bf16)


def fold_kernel(got, out, tmp):
    tmp[...] = jnp.sum(got[...].astype(f32), axis=0)
    nz = out.shape[0]
    per = tmp.shape[0] // nz
    for z in range(nz):
        out[z] = jnp.concatenate(
            [tmp[pl.ds(z, per, stride=nz), :], jnp.zeros((out.shape[1] - per, 128), f32)], axis=0
        ).astype(bf16)


def last_kernel(got, out):
    out[...] = jnp.sum(got[...].astype(f32), axis=0)[: out.shape[0]]


def up_kernel(ids, pair, *rest):
    pieces, out = rest[:-1], rest[-1]
    y, c = ids[0], ids[1]

    def put(yy, cc, val):
        out[:, pl.ds(pl.multiple_of((yy * 2 + cc) * 128, 128), 128)] = val.astype(f32)

    put(y, c, pair[0])
    put(y, 1 - c, pair[1])
    for i, rel in enumerate((3, 1, 2)):
        yy = lax.rem(y + rel, 4)
        put(yy, c, pieces[i][0])
        put(yy, 1 - c, pieces[i][1])


def layer(tokens, wq, wk, wv, down, lift, decay, grad):
    own, width = tokens.shape
    rank = lift.shape[1]
    heads = decay.shape[0]
    hk = wq.shape[1] // heads
    group = ("y", "c")
    ny, nz, nc, nx = (lax.axis_size(a) for a in ("y", "z", "c", "x"))
    ids = jnp.stack([lax.axis_index(a) for a in ("y", "c", "z")]).astype(jnp.int32)
    head = lax.axis_index("y") * nc + lax.axis_index("c")
    rows = wq.shape[0]
    span = nc * own
    ring = lambda v, s, a="y", n=ny: lax.ppermute(v, a, [(i, (i + s) % n) for i in range(n)])
    swap = lambda v: lax.ppermute(v, "c", [(0, 1), (1, 0)])
    DMA = pltpu.SemaphoreType.DMA

    below = ring(tokens, 1)
    above = ring(tokens, -1)
    far0 = ring(below[: own // 2], 1)
    far1 = ring(above[own // 2 :], -1)
    pieces = []
    for p in (tokens, below, above, far0, far1):
        pieces += [p, swap(p)]

    bundle = call(
        pack_kernel, shape((heads, 48 + rows, 3 * hk)), wk, wv, wq, grad, decay,
        specs=[HBM] * 5,
        mib=60,
        scratch=[pltpu.VMEM(wk.shape, bf16)] * 3
        + [pltpu.VMEM(grad.shape, bf16), pltpu.VMEM(decay.shape, f32), DMA((5,))],
    )
    bundle = lax.all_to_all(bundle, group, 0, 0, tiled=True)
    w = bundle[:, 48:].reshape(heads * rows, 3 * hk)
    weights, ahead, behind = [w], w, w
    for _ in range(nz // 2 - 1):
        ahead = ring(ahead, 1, "z", nz)
        behind = ring(behind, -1, "z", nz)
        weights += [ahead, behind]
    half = heads * rows // 2
    upper, lower = weights[3][:half], weights[4][half:]
    weights.append(ring(upper, 2, "z", nz))
    weights.append(ring(lower, -2, "z", nz))
    deep = nc * rows
    weights = [p.reshape(-1, deep, 3 * hk) for p in weights]

    logs = bundle[:, 32:35, 2 * hk :].astype(f32)
    logs = (logs[:, 0] + (logs[:, 1] + logs[:, 2])).reshape(ny, span)
    lift = lax.dynamic_slice_in_dim(lift, head * hk, hk, 2)
    zero = jnp.zeros((rank, hk), bf16)
    lift = jnp.stack([jnp.concatenate([lift[0], zero]), jnp.concatenate([zero, lift[1]])])

    kvql, qpre, tok, send = call(
        project_kernel,
        (
            shape((ny, 4, span, hk)), shape((ny, span, hk), f32),
            shape((heads, own, width)), shape((nz, 112, hk)),
        ),
        ids, down.reshape(ny, nz, deep, 2 * rank), *weights, *pieces, lift, logs,
        mib=60,
        specs=[SMEM] + [HBM] * 20 + [VMEM] * 2,
        out_specs=(HBM, HBM, HBM, VMEM),
        scratch=[
            pltpu.VMEM((ny, nz, deep, 3 * hk + 2 * rank), bf16),
            pltpu.VMEM((heads, own, width), bf16),
            pltpu.VMEM((ny, 4, span, hk), bf16),
            pltpu.VMEM((ny, span, hk), f32),
            pltpu.VMEM((ny, span, hk), f32),
            DMA((32,)),
        ],
    )

    got = lax.all_to_all(send, "z", 0, 0, tiled=True)
    scanned, gains = call(scan_fwd_kernel, (shape((nz, 96, hk)), shape((nz * ny, hk), f32)), got)
    s_in = lax.all_to_all(scanned, "z", 0, 0, tiled=True)

    send, back = call(
        attn_kernel,
        (shape((nz, 48, hk)), shape((ny, span, hk), f32)),
        s_in, lift, logs, kvql, qpre, bundle,
        mib=60,
        specs=[VMEM] * 3 + [HBM] * 3,
        out_specs=(VMEM, HBM),
        scratch=[
            pltpu.VMEM((ny, 4, span, hk), bf16),
            pltpu.VMEM((ny, span, hk), f32),
            pltpu.VMEM((heads, 48, 3 * hk), bf16),
            pltpu.VMEM((ny, span, hk), f32),
            DMA((4,)),
        ],
    )
    got = lax.all_to_all(send, "z", 0, 0, tiled=True)
    scanned = call(scan_bwd_kernel, shape((nz, 48, hk)), got, gains)
    r_in = lax.all_to_all(scanned, "z", 0, 0, tiled=True)

    out_rows = width // (ny * nz * nc * nx)
    down_terms, up = call(
        final_kernel,
        (shape((ny * nc * nx, nz * out_rows, hk)), shape((2 * rank, hk))),
        r_in, logs, kvql, back, tok,
        specs=[VMEM] * 2 + [HBM] * 3,
        scratch=[
            pltpu.VMEM((ny, span, hk), bf16),
            pltpu.VMEM((ny, span, hk), f32),
            pltpu.VMEM((heads, own, width), bf16),
            pltpu.VMEM((2 * rank, width), f32),
            pltpu.VMEM((width, 2 * rank), f32),
            DMA((10,)),
        ],
        mib=60,
    )
    down_terms = lax.all_to_all(down_terms, ("y", "c", "x"), 0, 0, tiled=True)
    pair = jnp.stack([up, swap(up)])
    ups = [ring(pair, 1), ring(pair, -1), ring(pair, 2)]
    down_terms = call(
        fold_kernel, shape((nz, 16, hk)), down_terms,
        scratch=[pltpu.VMEM((nz * out_rows, hk), f32)],
    )
    down_terms = lax.all_to_all(down_terms, "z", 0, 0, tiled=True)
    grad_down = call(last_kernel, shape((out_rows, hk), f32), down_terms)
    grad_up = call(
        up_kernel, shape((2 * rank, heads * hk), f32), ids, pair, *ups,
        specs=[SMEM] + [VMEM] * 4,
    )
    return (grad_down, grad_up.reshape(2, rank, heads * hk))


def solution(mesh):
    n_mp = mesh.shape["mp"]
    wide = Mesh(mesh.devices.reshape(4, 8, 2, n_mp), ("y", "z", "c", "x"))
    seq = ("y", "z", "c")
    return jax.shard_map(
        layer,
        mesh=wide,
        in_specs=(
            P(seq, None),
            P(seq, "x"),
            P(seq, "x"),
            P(seq, "x"),
            P(),
            P(None, None, "x"),
            P("x", seq),
            P(seq, "x"),
        ),
        out_specs=(P(("y", "z", "c", "x"), None), P(None, None, "x")),
        check_vma=False,
    )
```
